32 devices in a mesh: cols: 16 (over z, y, x), params: 2 (over core).
Axes of the slice: x: 2, y: 2, z: 4, core: 2. Of those that a mesh axis runs over, the one named last changes fastest.
Arguments:
- concentration: float32 [128, 16384], P(None, ('cols', 'params')), may hold values from 0.2 to 5
- emissions: float32 [128, 16384], P(None, ('cols', 'params')), may hold values from 0 to 1
- rate_table: float32 [8, 16, 16], replicated, may hold values from 0.01 to 0.3
- species_order: int32 [128], replicated, may hold values from 0 to 127, each once
- sensitivity: float32 [4, 128, 32, 4, 128], P('params', None, 'cols'), may hold values from -6 to 6
- source_terms: bfloat16 [4, 128, 32, 4, 128], P('params', None, 'cols'), may hold values from 0 to 2
- courant_x: float32 [32, 4, 128], P('cols'), may hold values from 0.05 to 0.24
- upwind_x: int32 [32, 4, 128], P('cols'), may hold values from 0 to 1
- courant_y: float32 [32, 4, 128], P('cols'), may hold values from 0.05 to 0.24
- upwind_y: int32 [32, 4, 128], P('cols'), may hold values from 0 to 1
Outputs:
- new_concentration: float32 [128, 16384], P(None, ('cols', 'params'))
- new_sensitivity: float32 [4, 128, 32, 4, 128], P('params', None, 'cols')
- sensitivity_burden: float32 [4, 128], P('params')
- species_burden: float32 [128], replicated
The draws below stay inside these ranges and needn't reach their ends.
Inputs may be any that keep to these rules, and one draw needn't show every extreme that they name: `species_order`: each species appears exactly once. `upwind_x`: 1 means the wind blows toward higher indices through the face. `upwind_y`: 1 means the wind blows toward higher indices through the face.
All inputs are finite; a program needn't handle non-finite values.
Results may differ from the reference program's by a relative error of at most 0.0016.
Values may be sent and summed in bfloat16 or wider, within the bound.
A program may use at most 128 MiB of HBM per device.

```python
import math
import jax
import jax.numpy as jnp
from jax import lax

SPECIES = 128
BLOCK = 16
LAYERS = 4
TY = 128
SUBSTEPS = 2
NBLOCK = 8
NPARAM = 4
NX = 32
NCELL = 16384


def touch_ends(values, rng, least, top_value):
    spot = [jax.random.randint(jax.random.fold_in(rng, axis), (), 0, length) for axis, length in enumerate(values.shape)]
    longest = values.shape.index(max(values.shape))
    beside = spot[:longest] + [(spot[longest] + 1) % values.shape[longest]] + spot[longest + 1:]
    return values.at[tuple(spot)].set(least).at[tuple(beside)].set(top_value)


def block_levels(key, dims, shards, smallest, largest):
    gain = 1.0
    for axis_at, blocks in shards:
        steps = jax.random.uniform(jax.random.fold_in(jax.random.fold_in(key, 6), axis_at), (blocks,), jnp.float32, smallest / len(shards), largest / len(shards))
        gain = gain * jnp.repeat(jnp.exp(steps), dims[axis_at] // blocks).reshape((-1,) + (1,) * (len(dims) - 1 - axis_at))
    return gain


def gaussian(stream_key, extent, width, bound, pieces=(), held_as=jnp.bfloat16):
    entries = width * jax.random.normal(stream_key, extent, jnp.float32)
    if pieces:
        entries = entries * block_levels(stream_key, extent, pieces, -0.22, 0.18)
    return jnp.clip(entries, -bound, bound).astype(held_as)


def setup_inputs(seed: int = 0) -> dict:
    seeds = jax.random.split(jax.random.key(seed), 11)
    return {
        "concentration": jnp.clip(jnp.exp(math.log(5.0) - 3.218876 * jax.random.uniform(seeds[0], (SPECIES, NCELL), jnp.float32) ** block_levels(seeds[0], (SPECIES, NCELL), ((1, 32),), -0.2, 0.2)), 0.2, 5.0),
        "emissions": jnp.clip(1.0 * jax.random.uniform(seeds[1], (SPECIES, NCELL), jnp.float32) ** block_levels(seeds[1], (SPECIES, NCELL), ((1, 32),), -0.2, 0.2), 0.0, 1.0),
        "rate_table": jnp.clip(jnp.exp(jax.random.uniform(seeds[2], (NBLOCK, BLOCK, BLOCK), jnp.float32, math.log(0.01), math.log(0.3))), 0.01, 0.3),
        "species_order": jax.random.permutation(seeds[3], SPECIES).astype(jnp.int32),
        "sensitivity": gaussian(seeds[4], (NPARAM, SPECIES, NX, LAYERS, TY), 1.0, 6.0, ((0, 2), (2, 16)), jnp.float32),
        "source_terms": jnp.clip(2.0 * jax.random.uniform(seeds[5], (NPARAM, SPECIES, NX, LAYERS, TY), jnp.float32) ** block_levels(seeds[5], (NPARAM, SPECIES, NX, LAYERS, TY), ((0, 2), (2, 16)), -0.2, 0.2), 0.0, 2.0).astype(jnp.bfloat16),
        "courant_x": jnp.clip(0.05 + 0.19 * jax.random.uniform(seeds[6], (NX, LAYERS, TY), jnp.float32) ** block_levels(seeds[6], (NX, LAYERS, TY), ((0, 16),), -0.2, 0.2), 0.05, 0.24),
        "upwind_x": touch_ends(jax.random.randint(seeds[7], (NX, LAYERS, TY), 0, 2), jax.random.fold_in(seeds[7], 1), 0, 1).astype(jnp.int32),
        "courant_y": jnp.clip(0.05 + 0.19 * jax.random.uniform(seeds[8], (NX, LAYERS, TY), jnp.float32) ** block_levels(seeds[8], (NX, LAYERS, TY), ((0, 16),), -0.2, 0.2), 0.05, 0.24),
        "upwind_y": touch_ends(jax.random.randint(seeds[9], (NX, LAYERS, TY), 0, 2), jax.random.fold_in(seeds[9], 1), 0, 1).astype(jnp.int32),
    }


def invert_blocks(matrix):
    size = matrix.shape[1]
    positions = jnp.arange(size)

    def eliminate(pivot_index, current):
        pivot = 1.0 / current[:, pivot_index, pivot_index, :]
        pivot_row = current[:, pivot_index, :, :] * pivot[:, None, :]
        pivot_row = jnp.where((positions == pivot_index)[None, :, None], pivot[:, None, :], pivot_row)
        column = current[:, :, pivot_index, :]
        updated = current - column[:, :, None, :] * pivot_row[:, None, :, :]
        updated = jnp.where((positions == pivot_index)[None, None, :, None], -column[:, :, None, :] * pivot[:, None, None, :], updated)
        updated = jnp.where((positions == pivot_index)[None, :, None, None], pivot_row[:, None, :, :], updated)
        return updated

    return lax.fori_loop(0, size, eliminate, matrix)


def build_factors(conc_cells, species_order, rate_table):
    block_count, block_width = rate_table.shape[0], rate_table.shape[1]
    ordered = jnp.take(conc_cells, species_order, axis=0).reshape(block_count, block_width, -1)
    coupling = rate_table[:, :, :, None] * ordered[:, None, :, :]
    row_total = jnp.sum(coupling, axis=2)
    positions = jnp.arange(block_width)
    identity = (positions[:, None] == positions[None, :]).astype(jnp.float32)
    system = identity[None, :, :, None] * (1.0 + row_total)[:, :, None, :] - coupling
    return invert_blocks(system).astype(jnp.bfloat16)


def apply_blocks(factors, values):
    result = jnp.zeros(values.shape, jnp.float32)
    for column_index in range(factors.shape[2]):
        result = result + factors[:, :, column_index, :].astype(jnp.float32)[None] * values[:, :, column_index, :][:, :, None, :]
    return result


def advect(tracer, courant_x, upwind_x, courant_y, upwind_y):
    before_x = jnp.concatenate([jnp.zeros_like(tracer[:, :, :1]), tracer[:, :, :-1]], axis=2)
    lower_x = courant_x * jnp.where(upwind_x == 1, before_x, -tracer)
    upper_x = jnp.concatenate([lower_x[:, :, 1:], jnp.zeros_like(lower_x[:, :, :1])], axis=2)
    before_y = jnp.concatenate([jnp.zeros_like(tracer[..., :1]), tracer[..., :-1]], axis=4)
    lower_y = courant_y * jnp.where(upwind_y == 1, before_y, -tracer)
    upper_y = jnp.concatenate([lower_y[..., 1:], jnp.zeros_like(lower_y[..., :1])], axis=4)
    return tracer + lower_x - upper_x + lower_y - upper_y


def reference(concentration, emissions, rate_table, species_order, sensitivity, source_terms, courant_x, upwind_x, courant_y, upwind_y):
    block_count = SPECIES // BLOCK
    plane_cells = LAYERS * TY
    tracer = sensitivity
    for substep in range(SUBSTEPS):
        tracer = advect(tracer, courant_x, upwind_x, courant_y, upwind_y)
    inverse = jnp.argsort(species_order).astype(jnp.int32)
    right_side = jnp.take(tracer + source_terms.astype(jnp.float32), species_order, axis=1)
    right_side = right_side.reshape(NPARAM, block_count, BLOCK, NX, plane_cells).transpose(3, 0, 1, 2, 4)
    base_side = jnp.take(concentration + emissions, species_order, axis=0)
    base_side = base_side.reshape(block_count, BLOCK, NX, plane_cells).transpose(2, 0, 1, 3)
    conc_planes = concentration.reshape(SPECIES, NX, plane_cells).transpose(1, 0, 2)

    def one_plane(items):
        conc_plane, base_plane, side_plane = items
        factors = build_factors(conc_plane, species_order, rate_table)
        return apply_blocks(factors, base_plane[None])[0], apply_blocks(factors, side_plane)

    new_base, new_tracer = lax.map(one_plane, (conc_planes, base_side, right_side))
    new_base = new_base.transpose(1, 2, 0, 3).reshape(SPECIES, NCELL)
    new_concentration = jnp.take(new_base, inverse, axis=0)
    new_tracer = new_tracer.transpose(1, 2, 3, 0, 4).reshape(NPARAM, SPECIES, NX, LAYERS, TY)
    new_sensitivity = jnp.take(new_tracer, inverse, axis=1)
    sensitivity_burden = jnp.sum(new_sensitivity, axis=(2, 3, 4)) / NCELL
    species_burden = jnp.sum(new_concentration, axis=1) / NCELL
    return new_concentration, new_sensitivity, sensitivity_burden, species_burden
```

```python
import functools
import jax
import jax.numpy as jnp
from jax import lax
from jax.experimental import pallas as pl
from jax.experimental.pallas import tpu as pltpu
from jax.sharding import PartitionSpec as P

MESH = pl.DeviceIdType.MESH
SUB = 8
PARTS = 2


def pinned(value):
    return pltpu.with_memory_space_constraint(value, pltpu.HBM)


def one_hot(column_ref):
    species = column_ref.shape[0]
    at = lax.broadcasted_iota(jnp.int32, (species, species), 1)
    return jnp.where(at == column_ref[...], 1.0, 0.0).astype(jnp.float32)


def exact_dot(left, right, over):
    return lax.dot_general(
        left, right, (over, ((), ())),
        precision=lax.Precision.HIGHEST, preferred_element_type=jnp.float32,
    )


def restore_kernel(order_ref, column_ref, newc_o, news_o, burd_o, newc_ref, news_ref, sburd_ref, cburd_ref):
    turn = one_hot(column_ref)
    newc_ref[...] = exact_dot(turn, newc_o[...], ((0,), (0,)))
    total = exact_dot(burd_o[...], turn, ((1,), (0,)))
    sburd_ref[...] = total[:2]
    cburd_ref[...] = total[2:3]

    @pl.loop(0, news_o.shape[1], unroll=8)
    def _(k):
        at = order_ref[k]
        for g in range(2):
            news_ref[g, at] = news_o[g, k]


def step_kernel(
    ncol, npar, blocks, width, total_cells,
    order_hbm, rate_hbm, conc_hbm, emis_hbm, sens_hbm, src_hbm, cx_hbm, ux_hbm, cy_hbm, uy_hbm,
    newc_ref, news_ref, burd_ref,
    order, rate, conc_ref, emis_ref, sens_ref, src_ref, cx_ref, ux_ref, cy_ref, uy_ref,
    conc_in, conc_rows, emis_rows, newc_rows, invc, lu, coef, wind, wind_in,
    send, halo, part, cpart, cpart_in, tot_out, tot_in,
    in_sem, conc_ssem, conc_rsem, w_ssem, w_rsem, p_ssem, p_rsem, f_ssem, f_rsem, cp_ssem, cp_rsem, t_ssem, t_rsem,
):
    species = blocks * width
    part_width = width // PARTS
    chunks = blocks * PARTS
    half = SUB // 2
    col, par = (lax.axis_index("cols"), lax.axis_index("params"))
    rows = conc_ref.shape[1] // 128
    has_left, has_right = (col > 0, col < ncol - 1)
    odd = lax.rem(col, 2)
    other = 1 - odd
    partner = col + 1 - 2 * odd
    ahead = col + 2 - 4 * odd
    forwards = jnp.logical_and(ahead >= 0, ahead < ncol)
    ahead = jnp.clip(ahead, 0, ncol - 1)
    behind = col - 2 + 4 * odd
    receives = jnp.logical_and(behind >= 0, behind < ncol)

    barrier = pltpu.get_barrier_semaphore()
    for d in range(1, ncol):
        pl.semaphore_signal(barrier, inc=1, device_id=(lax.rem(col + d, ncol), par), device_id_type=MESH)
    for d in range(1, npar):
        pl.semaphore_signal(barrier, inc=1, device_id=(col, lax.rem(par + d, npar)), device_id_type=MESH)

    held = (
        (order_hbm, order), (sens_hbm, sens_ref), (cx_hbm, cx_ref), (ux_hbm, ux_ref), (cy_hbm, cy_ref), (uy_hbm, uy_ref),
        (conc_hbm, conc_ref), (emis_hbm, emis_ref), (rate_hbm, rate), (src_hbm, src_ref),
    )
    loads = [pltpu.make_async_copy(src, dst, in_sem.at[n]) for n, (src, dst) in enumerate(held)]
    for load in loads:
        load.start()

    row = lax.broadcasted_iota(jnp.int32, (SUB, 128), 0)
    lane = lax.broadcasted_iota(jnp.int32, (SUB, 128), 1)
    top = row < half

    @pl.when(jnp.logical_not(has_left))
    def _():
        halo[0] = jnp.zeros_like(halo[0])
        wind_in[0] = jnp.zeros_like(wind_in[0])

    @pl.when(jnp.logical_not(has_right))
    def _():
        halo[1] = jnp.zeros_like(halo[1])
        wind_in[1] = jnp.zeros_like(wind_in[1])

    def wind_copy(way):
        target = jnp.minimum(col + 1, ncol - 1) if way == 0 else jnp.maximum(col - 1, 0)
        return pltpu.make_async_remote_copy(
            src_ref=wind, dst_ref=wind_in.at[way], send_sem=w_ssem.at[way], recv_sem=w_rsem.at[way],
            device_id=(target, par), device_id_type=MESH,
        )

    def pair_copy(n, side):
        return pltpu.make_async_remote_copy(
            src_ref=send.at[n], dst_ref=halo.at[side, n], send_sem=p_ssem.at[n], recv_sem=p_rsem.at[n],
            device_id=(partner, par), device_id_type=MESH,
        )

    def forward_copy(n):
        return pltpu.make_async_remote_copy(
            src_ref=halo.at[other, n], dst_ref=halo.at[odd, n], send_sem=f_ssem.at[n], recv_sem=f_rsem.at[n],
            device_id=(ahead, par), device_id_type=MESH,
        )

    def pass_on(n):
        pair_copy(n, other).wait_recv()

        @pl.when(forwards)
        def _():
            forward_copy(n).start()

    def pack(n):
        for k in range(part_width):
            at = order[n * part_width + k]
            both = jnp.concatenate([sens_ref[0, at], sens_ref[1, at]], axis=0)
            send[n, k] = both.astype(jnp.bfloat16)

    loads[0].wait()
    loads[1].wait()
    pack(0)
    for load in loads[2:6]:
        load.wait()
    wind[0] = jnp.where(ux_ref[...] == 1, cx_ref[...], -cx_ref[...])
    wind[1] = jnp.where(uy_ref[...] == 1, cy_ref[...], -cy_ref[...])
    loads[6].wait()
    pl.semaphore_wait(barrier, ncol - 1 + npar - 1)
    pair_copy(0, odd).start()

    @pl.when(has_right)
    def _():
        wind_copy(0).start()

    @pl.when(has_left)
    def _():
        wind_copy(1).start()

    conc_copies = []
    for d in range(1, npar):
        copy = pltpu.make_async_remote_copy(
            src_ref=conc_ref, dst_ref=conc_in.at[npar - 1 - d],
            send_sem=conc_ssem.at[d - 1], recv_sem=conc_rsem.at[npar - 1 - d],
            device_id=(col, lax.rem(par + d, npar)), device_id_type=MESH,
        )
        copy.start()
        conc_copies.append(copy)

    @pl.loop(1, chunks)
    def _(n):
        pack(n)
        pair_copy(n, odd).start()

    def spread(read, target, base):
        target = target.reshape(species * SUB, 128)

        @pl.loop(0, species // SUB)
        def _(t):
            for r in range(rows):
                target[pl.ds(t * SUB * SUB + base + r, SUB, stride=SUB), :] = read(t, r)

    def own(ref):
        return lambda t, r: ref[pl.ds(pl.multiple_of(t * SUB, SUB), SUB), r * 128:(r + 1) * 128]

    spread(own(conc_ref), conc_rows, par * rows)
    loads[7].wait()
    spread(own(emis_ref), emis_rows, par * rows)
    loads[8].wait()
    loads[9].wait()

    def set_coefficients():
        @pl.when(has_left)
        def _():
            wind_copy(0).wait_recv()

        @pl.when(has_right)
        def _():
            wind_copy(1).wait_recv()

        zero = jnp.zeros((SUB, 128), jnp.float32)

        def split(value):
            return (jnp.maximum(value, zero), jnp.maximum(-value, zero))

        def swap(value):
            return pltpu.roll(value, half, 0)

        def across(value):
            into, out = split(value)
            last = lane == 127
            next_in = jnp.where(last, zero, pltpu.roll(into, 127, 1))
            next_out = jnp.where(last, zero, pltpu.roll(out, 127, 1))
            return (out + next_in, jnp.where(lane == 0, zero, into), next_out)

        own_x, left_x, right_x = (wind[0], wind_in[0, 0], wind_in[1, 0])
        in_x, out_x = split(own_x)
        next_in, next_out = split(jnp.where(top, swap(own_x), swap(right_x)))
        lost, down, up = across(wind[1])
        coef[0] = 1.0 - (out_x + next_in) - lost
        coef[1] = jnp.where(jnp.logical_and(top, jnp.logical_not(has_left)), zero, in_x)
        coef[2] = next_out
        coef[3] = down
        coef[4] = up
        in_x, out_x = split(jnp.where(top, swap(left_x), swap(right_x)))
        next_in, next_out = split(jnp.where(top, own_x, right_x))
        lost, down, up = across(jnp.where(top, swap(wind_in[0, 1]), swap(wind_in[1, 1])))
        coef[5] = 1.0 - (out_x + next_in) - lost
        coef[6] = in_x
        coef[7] = next_out
        coef[8] = down
        coef[9] = up

    def stencil(first, value, before, after):
        a0, al, ar, ad, au = (coef[first + n] for n in range(5))
        return (
            a0 * value + al * before + ar * after
            + ad * pltpu.roll(value, 1, 1) + au * pltpu.roll(value, 127, 1)
        )

    def advance(s, h):
        turned = pltpu.roll(s, half, 0)
        return stencil(0, s, jnp.where(top, h, turned), jnp.where(top, turned, h))

    def transport(s, left, right):
        h = pltpu.roll(jnp.where(top, right, left), half, 0)
        next_h = stencil(5, h, jnp.where(top, left, s), jnp.where(top, s, right))
        return advance(advance(s, h), next_h)

    for d in range(1, npar):
        conc_copies[npar - 1 - d].wait_recv()
        spread(own(conc_in.at[d - 1]), conc_rows, lax.rem(par + d, npar) * rows)

    set_coefficients()

    def factorize(b):
        c = [conc_rows[order[b * width + j]] for j in range(width)]
        for i in range(width):
            invc[b, i] = 1.0 / c[i]

        def fresh(i):
            rates = [rate[b, i, j] for j in range(width)]
            total = rates[0] * c[0]
            for j in range(1, width):
                total = total + rates[j] * c[j]
            diagonal = (1.0 + total) * invc[b, i] - rates[i]
            return [diagonal if j == i else jnp.full((SUB, 128), -rates[j], jnp.float32) for j in range(width)]

        for i in range(0, width, 2):
            x, y = (fresh(i), fresh(i + 1))
            for k in range(i):
                inv = lu[b, k, k]
                lx, ly = (x[k] * inv, y[k] * inv)
                lu[b, i, k] = lx
                lu[b, i + 1, k] = ly
                for j in range(k + 1, width):
                    u = lu[b, k, j]
                    x[j] = x[j] - lx * u
                    y[j] = y[j] - ly * u
            inv = 1.0 / x[i]
            lu[b, i, i] = inv
            ly = y[i] * inv
            lu[b, i + 1, i] = ly
            for j in range(i + 1, width):
                lu[b, i, j] = x[j]
                y[j] = y[j] - ly * x[j]
            lu[b, i + 1, i + 1] = 1.0 / y[i + 1]
            for j in range(i + 2, width):
                lu[b, i + 1, j] = y[j]

    def solve(b, sides):
        sides = [list(side) for side in sides]
        for k in range(width):
            for i in range(k + 1, width):
                low = lu[b, i, k]
                for side in sides:
                    side[i] = side[i] - low * side[k]
        for k in range(width - 1, -1, -1):
            inv = lu[b, k, k]
            for side in sides:
                side[k] = side[k] * inv
            for i in range(k):
                up = lu[b, i, k]
                for side in sides:
                    side[i] = side[i] - up * side[k]
        return [[side[k] * invc[b, k] for k in range(width)] for side in sides]

    @pl.loop(0, blocks)
    def _(b):
        factorize(b)
        pass_on(b)
        base = []
        for k in range(width):
            at = order[b * width + k]
            base.append(conc_rows[at] + emis_rows[at])
        (base,) = solve(b, [base])
        for k in range(width):
            o = b * width + k
            newc_rows[pl.ds(pl.multiple_of(o * SUB, SUB), SUB), :] = base[k]

    @pl.loop(0, species // SUB)
    def _(t):
        total = jnp.zeros((SUB, 128), jnp.float32)
        at = pl.ds(pl.multiple_of(t * SUB, SUB), SUB)
        for r in range(rows):
            value = newc_rows[pl.ds(t * SUB * SUB + par * rows + r, SUB, stride=SUB), :]
            newc_ref[at, r * 128:(r + 1) * 128] = value
            total = total + value
        part[0, at, :] = total

    ones = jnp.ones((SUB, 128), jnp.float32)

    def lane_sums(value):
        return lax.dot_general(
            ones, value, (((1,), (1,)), ((), ())),
            precision=lax.Precision.HIGHEST, preferred_element_type=jnp.float32,
        )

    own_c = lane_sums(part[0])
    cpart[...] = own_c
    cpart_in[par] = own_c

    def cpart_copy(d):
        return pltpu.make_async_remote_copy(
            src_ref=cpart, dst_ref=cpart_in.at[par],
            send_sem=cp_ssem.at[d - 1], recv_sem=cp_rsem.at[d - 1],
            device_id=(col, lax.rem(par + d, npar)), device_id_type=MESH,
        )

    for d in range(1, npar):
        cpart_copy(d).start()

    def second_half(b):
        sides = [[], []]
        for k in range(width):
            at = order[b * width + k]
            n, m = (b * PARTS + k // part_width, k % part_width)
            left, right = (halo[0, n, m].astype(jnp.float32), halo[1, n, m].astype(jnp.float32))
            for g in range(2):
                rows_g = slice(g * SUB, (g + 1) * SUB)
                moved = transport(sens_ref[g, at], left[rows_g], right[rows_g])
                sides[g].append(moved + src_ref[g, at].astype(jnp.float32))
        sides = solve(b, sides)
        for g in range(2):
            for k in range(width):
                at = (g * species + b * width + k) * SUB
                news_ref[pl.ds(pl.multiple_of(at, SUB), SUB), :] = sides[g][k]

    @pl.loop(0, blocks)
    def _(b):
        for n in range(PARTS - 1):
            pass_on(blocks + b * (PARTS - 1) + n)

        @pl.when(receives)
        def _():
            for n in range(PARTS):
                forward_copy(b * PARTS + n).wait_recv()

        second_half(b)

    @pl.loop(0, species // SUB)
    def _(t):
        at = pl.ds(pl.multiple_of(t * SUB, SUB), SUB)
        for g in range(2):
            total = jnp.zeros((SUB, 128), jnp.float32)
            for r in range(SUB):
                total = total + news_ref[pl.ds(g * species * SUB + t * SUB * SUB + r, SUB, stride=SUB), :]
            part[1 + g, at, :] = total

    for d in range(1, npar):
        cpart_copy(d).wait()
    c_total = cpart_in[0]
    for q in range(1, npar):
        c_total = c_total + cpart_in[q]
    sums = [lane_sums(part[1 + g]) for g in range(2)]
    result = jnp.where(row == 0, sums[0], jnp.where(row == 1, sums[1], c_total))
    tot_out[...] = result
    tot_in[col] = result
    totals = []
    for d in range(1, ncol):
        copy = pltpu.make_async_remote_copy(
            src_ref=tot_out, dst_ref=tot_in.at[col],
            send_sem=t_ssem.at[d - 1], recv_sem=t_rsem.at[d - 1],
            device_id=(lax.rem(col + d, ncol), par), device_id_type=MESH,
        )
        copy.start()
        totals.append(copy)
    for d in range(1, npar):
        conc_copies[d - 1].wait_send()

    @pl.when(has_right)
    def _():
        wind_copy(0).wait_send()

    @pl.when(has_left)
    def _():
        wind_copy(1).wait_send()

    @pl.loop(0, chunks)
    def _(n):
        pair_copy(n, odd).wait_send()

        @pl.when(forwards)
        def _():
            forward_copy(n).wait_send()

    for copy in totals:
        copy.wait()
    total = tot_in[0]
    for q in range(1, ncol):
        total = total + tot_in[q]
    total = total / total_cells
    burd_ref[...] = total


def shards(
    concentration, emissions, rate_table, species_order, sensitivity, source_terms,
    courant_x, upwind_x, courant_y, upwind_y,
):
    ncol, npar = (lax.axis_size("cols"), lax.axis_size("params"))
    blocks, width = (rate_table.shape[0], rate_table.shape[1])
    groups, species, planes, layers, across = sensitivity.shape
    tall = planes * layers
    assert ncol % 2 == 0 and groups == 2 and tall == SUB and planes == 2 and across == 128
    cells = tall * across

    vm = pltpu.VMEM
    dma = pltpu.SemaphoreType.DMA
    rows_shape = (species * SUB, 128)
    in_vmem = pl.BlockSpec(memory_space=pltpu.VMEM)
    in_smem = pl.BlockSpec(memory_space=pltpu.SMEM)
    order_column = species_order.reshape(species, 1)
    limits = pltpu.CompilerParams(vmem_limit_bytes=16 * 1024 * 1024)
    stacked = (groups, species, SUB, across)
    chunks = blocks * PARTS
    packed_shape = (chunks, width // PARTS, 2 * SUB, 128)
    newc_o, news_o, burd_o = pl.pallas_call(
        functools.partial(step_kernel, ncol, npar, blocks, width, cells * ncol),
        out_shape=(
            jax.ShapeDtypeStruct(concentration.shape, jnp.float32),
            jax.ShapeDtypeStruct((groups * species * SUB, 128), jnp.float32),
            jax.ShapeDtypeStruct((SUB, species), jnp.float32),
        ),
        in_specs=[pl.BlockSpec(memory_space=pltpu.HBM)] * 10,
        out_specs=[in_vmem] * 3,
        scratch_shapes=[
            pltpu.SMEM((species,), jnp.int32),
            pltpu.SMEM(rate_table.shape, jnp.float32),
            vm(concentration.shape, jnp.float32),
            vm(concentration.shape, jnp.float32),
            vm(stacked, jnp.float32),
            vm(stacked, jnp.bfloat16),
            vm((SUB, 128), jnp.float32),
            vm((SUB, 128), jnp.int32),
            vm((SUB, 128), jnp.float32),
            vm((SUB, 128), jnp.int32),
            vm((npar - 1,) + concentration.shape, jnp.float32),
            vm((species, SUB, 128), jnp.float32),
            vm((species, SUB, 128), jnp.float32),
            vm(rows_shape, jnp.float32),
            vm((blocks, width, SUB, 128), jnp.float32),
            vm((blocks, width, width, SUB, 128), jnp.float32),
            vm((10, SUB, 128), jnp.float32),
            vm((2, SUB, 128), jnp.float32),
            vm((2, 2, SUB, 128), jnp.float32),
            vm(packed_shape, jnp.bfloat16),
            vm((2,) + packed_shape, jnp.bfloat16),
            vm((3, species, 128), jnp.float32),
            vm((SUB, species), jnp.float32),
            vm((npar, SUB, species), jnp.float32),
            vm((SUB, species), jnp.float32),
            vm((ncol, SUB, species), jnp.float32),
            dma((10,)),
            dma((npar - 1,)), dma((npar - 1,)),
            dma((2,)), dma((2,)),
            dma((chunks,)), dma((chunks,)),
            dma((chunks,)), dma((chunks,)),
            dma((npar - 1,)), dma((npar - 1,)),
            dma((ncol - 1,)), dma((ncol - 1,)),
        ],
        compiler_params=pltpu.CompilerParams(
            collective_id=0, has_side_effects=True, vmem_limit_bytes=48 * 1024 * 1024
        ),
    )(
        pinned(species_order), pinned(rate_table), pinned(concentration), pinned(emissions),
        pinned(sensitivity.reshape(stacked)), pinned(source_terms.reshape(stacked)),
        pinned(courant_x.reshape(SUB, across)), pinned(upwind_x.reshape(SUB, across)),
        pinned(courant_y.reshape(SUB, across)), pinned(upwind_y.reshape(SUB, across)),
    )
    newc, news, sburd, cburd = pl.pallas_call(
        restore_kernel,
        out_shape=(
            jax.ShapeDtypeStruct(concentration.shape, jnp.float32),
            jax.ShapeDtypeStruct(stacked, jnp.float32),
            jax.ShapeDtypeStruct((groups, species), jnp.float32),
            jax.ShapeDtypeStruct((1, species), jnp.float32),
        ),
        in_specs=[in_smem] + [in_vmem] * 4,
        out_specs=[in_vmem] * 4,
        compiler_params=limits,
    )(species_order, order_column, newc_o, news_o.reshape(stacked), burd_o)
    return (newc, news.reshape(sensitivity.shape), sburd, cburd.reshape(species))


def solution(mesh):
    in_specs = (
        P(None, ("cols", "params")),
        P(None, ("cols", "params")),
        P(),
        P(),
        P("params", None, "cols", None, None),
        P("params", None, "cols", None, None),
        P("cols", None, None),
        P("cols", None, None),
        P("cols", None, None),
        P("cols", None, None),
    )
    out_specs = (
        P(None, ("cols", "params")),
        P("params", None, "cols", None, None),
        P("params", None),
        P(),
    )
    return jax.shard_map(shards, mesh=mesh, in_specs=in_specs, out_specs=out_specs, check_vma=False)
```

```python
import functools
import jax
import jax.numpy as jnp
from jax import lax
from jax.experimental import pallas as pl
from jax.experimental.pallas import tpu as pltpu
from jax.sharding import PartitionSpec as P

MESH = pl.DeviceIdType.MESH
SUB = 8
PARTS = 2
LAG = 4


def pinned(value):
    return pltpu.with_memory_space_constraint(value, pltpu.HBM)


def restore_kernel(order, order_row, newc_o, news_o, burd_o, newc_hbm, news_hbm, sburd_ref, cburd_ref, news_ref, newc_rows, newc_ref, sems):
    species = news_o.shape[1]
    rows = newc_ref.shape[1] // 128
    first = lax.axis_index("params") * rows

    def put(group):
        @pl.loop(0, species, unroll=8)
        def _(k):
            news_ref[group, order[0, k]] = news_o[group, k]

        copy = pltpu.make_async_copy(news_ref.at[group], news_hbm.at[group], sems.at[group])
        copy.start()
        return copy

    copies = [put(0), put(1)]

    @pl.loop(0, species, unroll=8)
    def _(k):
        newc_rows[order[0, k]] = newc_o[k]

    flat = newc_rows.reshape(species * SUB, 128)
    for t in range(species // SUB):
        for r in range(rows):
            newc_ref[t * SUB:(t + 1) * SUB, r * 128:(r + 1) * 128] = flat[pl.ds(t * SUB * SUB + first + r, SUB, stride=SUB), :]
    copies.append(pltpu.make_async_copy(newc_ref, newc_hbm, sems.at[2]))
    copies[2].start()
    at = lax.broadcasted_iota(jnp.int32, (species, species), 0)
    turn = jnp.where(at == order_row[...], 1.0, 0.0).astype(jnp.float32)
    total = lax.dot_general(
        burd_o[...], turn, (((1,), (1,)), ((), ())),
        precision=lax.Precision.HIGHEST, preferred_element_type=jnp.float32,
    )
    sburd_ref[...] = total[:2]
    cburd_ref[...] = total[2:3]
    for copy in copies:
        copy.wait()


def step_kernel(
    ncol, npar, blocks, width, total_cells,
    order_hbm, rate_hbm, conc_hbm, emis_hbm, sens_hbm, src_hbm, cx_hbm, ux_hbm, cy_hbm, uy_hbm,
    newc_ref, news_ref, burd_ref, order_out,
    order, rate, conc_ref, emis_ref, sens_ref, src_ref, cx_ref, ux_ref, cy_ref, uy_ref,
    conc_in, conc_rows, emis_rows, invc, lu, coef, wind, wind_in,
    send, halo, part, cpart, cpart_in, tot_out, tot_in,
    in_sem, conc_ssem, conc_rsem, w_ssem, w_rsem, p_ssem, p_rsem, f_ssem, f_rsem, cp_ssem, cp_rsem, t_ssem, t_rsem,
):
    species = blocks * width
    part_width = width // PARTS
    chunks = blocks * PARTS
    half = SUB // 2
    col, par = (lax.axis_index("cols"), lax.axis_index("params"))
    rows = conc_ref.shape[1] // 128
    has_left, has_right = (col > 0, col < ncol - 1)
    odd = lax.rem(col, 2)
    other = 1 - odd
    partner = col + 1 - 2 * odd
    ahead = col + 2 - 4 * odd
    forwards = jnp.logical_and(ahead >= 0, ahead < ncol)
    ahead = jnp.clip(ahead, 0, ncol - 1)
    behind = col - 2 + 4 * odd
    receives = jnp.logical_and(behind >= 0, behind < ncol)

    barrier = pltpu.get_barrier_semaphore()
    for d in range(1, ncol):
        pl.semaphore_signal(barrier, inc=1, device_id=(lax.rem(col + d, ncol), par), device_id_type=MESH)
    for d in range(1, npar):
        pl.semaphore_signal(barrier, inc=1, device_id=(col, lax.rem(par + d, npar)), device_id_type=MESH)

    held = (
        (order_hbm, order), (sens_hbm, sens_ref), (cx_hbm, cx_ref), (ux_hbm, ux_ref), (cy_hbm, cy_ref), (uy_hbm, uy_ref),
        (conc_hbm, conc_ref), (emis_hbm, emis_ref), (rate_hbm, rate), (src_hbm, src_ref), (order_hbm, order_out),
    )
    loads = [pltpu.make_async_copy(src, dst, in_sem.at[n]) for n, (src, dst) in enumerate(held)]
    for load in loads:
        load.start()

    row = lax.broadcasted_iota(jnp.int32, (SUB, 128), 0)
    lane = lax.broadcasted_iota(jnp.int32, (SUB, 128), 1)
    top = row < half

    @pl.when(jnp.logical_not(has_left))
    def _():
        halo[0] = jnp.zeros_like(halo[0])
        wind_in[0] = jnp.zeros_like(wind_in[0])

    @pl.when(jnp.logical_not(has_right))
    def _():
        halo[1] = jnp.zeros_like(halo[1])
        wind_in[1] = jnp.zeros_like(wind_in[1])

    def wind_copy(way):
        target = jnp.minimum(col + 1, ncol - 1) if way == 0 else jnp.maximum(col - 1, 0)
        return pltpu.make_async_remote_copy(
            src_ref=wind, dst_ref=wind_in.at[way], send_sem=w_ssem.at[way], recv_sem=w_rsem.at[way],
            device_id=(target, par), device_id_type=MESH,
        )

    def pair_copy(n, side):
        return pltpu.make_async_remote_copy(
            src_ref=send.at[n], dst_ref=halo.at[side, n], send_sem=p_ssem.at[n], recv_sem=p_rsem.at[n],
            device_id=(partner, par), device_id_type=MESH,
        )

    def forward_copy(n):
        return pltpu.make_async_remote_copy(
            src_ref=halo.at[other, n], dst_ref=halo.at[odd, n], send_sem=f_ssem.at[n], recv_sem=f_rsem.at[n],
            device_id=(ahead, par), device_id_type=MESH,
        )

    def pass_on(n):
        pair_copy(n, other).wait_recv()

        @pl.when(forwards)
        def _():
            forward_copy(n).start()

    def pack(n):
        for k in range(part_width):
            at = order[0, n * part_width + k]
            both = jnp.concatenate([sens_ref[0, at], sens_ref[1, at]], axis=0)
            send[n, k] = both.astype(jnp.bfloat16)

    for load in loads[2:6]:
        load.wait()
    wind[0] = jnp.where(ux_ref[...] == 1, cx_ref[...], -cx_ref[...])
    wind[1] = jnp.where(uy_ref[...] == 1, cy_ref[...], -cy_ref[...])
    loads[6].wait()
    loads[0].wait()
    loads[1].wait()
    pack(0)
    pl.semaphore_wait(barrier, ncol - 1 + npar - 1)
    conc_copies = []
    for d in range(1, npar):
        copy = pltpu.make_async_remote_copy(
            src_ref=conc_ref, dst_ref=conc_in.at[npar - 1 - d],
            send_sem=conc_ssem.at[d - 1], recv_sem=conc_rsem.at[npar - 1 - d],
            device_id=(col, lax.rem(par + d, npar)), device_id_type=MESH,
        )
        copy.start()
        conc_copies.append(copy)
    pair_copy(0, odd).start()

    @pl.when(has_right)
    def _():
        wind_copy(0).start()

    @pl.when(has_left)
    def _():
        wind_copy(1).start()

    @pl.loop(1, chunks)
    def _(n):
        pack(n)
        pair_copy(n, odd).start()

    def spread(read, target, base):
        target = target.reshape(species * SUB, 128)

        @pl.loop(0, species // SUB)
        def _(t):
            for r in range(rows):
                target[pl.ds(t * SUB * SUB + base + r, SUB, stride=SUB), :] = read(t, r)

    def own(ref):
        return lambda t, r: ref[pl.ds(pl.multiple_of(t * SUB, SUB), SUB), r * 128:(r + 1) * 128]

    spread(own(conc_ref), conc_rows, par * rows)
    loads[7].wait()
    spread(own(emis_ref), emis_rows, par * rows)
    for load in loads[8:]:
        load.wait()

    def set_coefficients():
        @pl.when(has_left)
        def _():
            wind_copy(0).wait_recv()

        @pl.when(has_right)
        def _():
            wind_copy(1).wait_recv()

        zero = jnp.zeros((SUB, 128), jnp.float32)

        def split(value):
            return (jnp.maximum(value, zero), jnp.maximum(-value, zero))

        def swap(value):
            return pltpu.roll(value, half, 0)

        def across(value):
            into, out = split(value)
            last = lane == 127
            next_in = jnp.where(last, zero, pltpu.roll(into, 127, 1))
            next_out = jnp.where(last, zero, pltpu.roll(out, 127, 1))
            return (out + next_in, jnp.where(lane == 0, zero, into), next_out)

        own_x, left_x, right_x = (wind[0], wind_in[0, 0], wind_in[1, 0])
        in_x, out_x = split(own_x)
        next_in, next_out = split(jnp.where(top, swap(own_x), swap(right_x)))
        lost, down, up = across(wind[1])
        coef[0] = 1.0 - (out_x + next_in) - lost
        coef[1] = jnp.where(jnp.logical_and(top, jnp.logical_not(has_left)), zero, in_x)
        coef[2] = next_out
        coef[3] = down
        coef[4] = up
        in_x, out_x = split(jnp.where(top, swap(left_x), swap(right_x)))
        next_in, next_out = split(jnp.where(top, own_x, right_x))
        lost, down, up = across(jnp.where(top, swap(wind_in[0, 1]), swap(wind_in[1, 1])))
        coef[5] = 1.0 - (out_x + next_in) - lost
        coef[6] = in_x
        coef[7] = next_out
        coef[8] = down
        coef[9] = up

    def stencil(first, value, before, after):
        a0, al, ar, ad, au = (coef[first + n] for n in range(5))
        return (
            a0 * value + al * before + ar * after
            + ad * pltpu.roll(value, 1, 1) + au * pltpu.roll(value, 127, 1)
        )

    def advance(s, h):
        turned = pltpu.roll(s, half, 0)
        return stencil(0, s, jnp.where(top, h, turned), jnp.where(top, turned, h))

    def transport(s, left, right):
        h = pltpu.roll(jnp.where(top, right, left), half, 0)
        next_h = stencil(5, h, jnp.where(top, left, s), jnp.where(top, s, right))
        return advance(advance(s, h), next_h)

    for d in range(1, npar):
        conc_copies[npar - 1 - d].wait_recv()
        spread(own(conc_in.at[d - 1]), conc_rows, lax.rem(par + d, npar) * rows)

    set_coefficients()

    def factorize(b):
        c = [conc_rows[order[0, b * width + j]] for j in range(width)]
        for i in range(width):
            invc[b, i] = 1.0 / c[i]

        def fresh(i):
            rates = [rate[b, i, j] for j in range(width)]
            total = rates[0] * c[0]
            for j in range(1, width):
                total = total + rates[j] * c[j]
            diagonal = (1.0 + total) * invc[b, i] - rates[i]
            return [diagonal if j == i else jnp.full((SUB, 128), -rates[j], jnp.float32) for j in range(width)]

        for i in range(0, width, 2):
            x, y = (fresh(i), fresh(i + 1))
            for k in range(i):
                inv = lu[b, k, k]
                lx, ly = (x[k] * inv, y[k] * inv)
                lu[b, i, k] = lx
                lu[b, i + 1, k] = ly
                for j in range(k + 1, width):
                    u = lu[b, k, j]
                    x[j] = x[j] - lx * u
                    y[j] = y[j] - ly * u
            inv = 1.0 / x[i]
            lu[b, i, i] = inv
            ly = y[i] * inv
            lu[b, i + 1, i] = ly
            for j in range(i + 1, width):
                lu[b, i, j] = x[j]
                y[j] = y[j] - ly * x[j]
            lu[b, i + 1, i + 1] = 1.0 / y[i + 1]
            for j in range(i + 2, width):
                lu[b, i + 1, j] = y[j]

    def solve(b, sides):
        sides = [list(side) for side in sides]
        for k in range(width):
            for i in range(k + 1, width):
                low = lu[b, i, k]
                for side in sides:
                    side[i] = side[i] - low * side[k]
        for k in range(width - 1, -1, -1):
            inv = lu[b, k, k]
            for side in sides:
                side[k] = side[k] * inv
            for i in range(k):
                up = lu[b, i, k]
                for side in sides:
                    side[i] = side[i] - up * side[k]
        return [[side[k] * invc[b, k] for k in range(width)] for side in sides]

    def first_half(b):
        factorize(b)
        base = []
        for k in range(width):
            at = order[0, b * width + k]
            base.append(conc_rows[at] + emis_rows[at])
        (base,) = solve(b, [base])
        for k in range(width):
            o = b * width + k
            newc_ref[pl.ds(pl.multiple_of(o * SUB, SUB), SUB), :] = base[k]

    def second_half(b):
        sides = [[], []]
        for k in range(width):
            at = order[0, b * width + k]
            n, m = (b * PARTS + k // part_width, k % part_width)
            left, right = (halo[0, n, m].astype(jnp.float32), halo[1, n, m].astype(jnp.float32))
            for g in range(2):
                rows_g = slice(g * SUB, (g + 1) * SUB)
                moved = transport(sens_ref[g, at], left[rows_g], right[rows_g])
                sides[g].append(moved + src_ref[g, at].astype(jnp.float32))
        sides = solve(b, sides)
        for g in range(2):
            for k in range(width):
                at = (g * species + b * width + k) * SUB
                news_ref[pl.ds(pl.multiple_of(at, SUB), SUB), :] = sides[g][k]
        for g in range(2):
            for t in range(width // SUB):
                first = b * width + t * SUB
                total = jnp.zeros((SUB, 128), jnp.float32)
                for r in range(SUB):
                    total = total + news_ref[pl.ds((g * species + first) * SUB + r, SUB, stride=SUB), :]
                part[1 + g, pl.ds(pl.multiple_of(first, SUB), SUB), :] = total

    @pl.loop(0, blocks + LAG)
    def _(step):
        @pl.when(step < blocks)
        def _():
            first_half(step)

        @pl.when(jnp.logical_and(step >= 1, step <= blocks))
        def _():
            for n in range(PARTS):
                pass_on((step - 1) * PARTS + n)

        @pl.when(step >= LAG)
        def _():
            b = step - LAG

            @pl.when(receives)
            def _():
                for n in range(PARTS):
                    forward_copy(b * PARTS + n).wait_recv()

            second_half(b)

    @pl.loop(0, species // SUB)
    def _(t):
        total = jnp.zeros((SUB, 128), jnp.float32)
        at = pl.ds(pl.multiple_of(t * SUB, SUB), SUB)
        for r in range(rows):
            total = total + newc_ref[pl.ds(t * SUB * SUB + par * rows + r, SUB, stride=SUB), :]
        part[0, at, :] = total

    ones = jnp.ones((SUB, 128), jnp.float32)

    def lane_sums(value):
        return lax.dot_general(
            ones, value, (((1,), (1,)), ((), ())),
            precision=lax.Precision.HIGHEST, preferred_element_type=jnp.float32,
        )

    own_c = lane_sums(part[0])
    cpart[...] = own_c
    cpart_in[par] = own_c

    def cpart_copy(d):
        return pltpu.make_async_remote_copy(
            src_ref=cpart, dst_ref=cpart_in.at[par],
            send_sem=cp_ssem.at[d - 1], recv_sem=cp_rsem.at[d - 1],
            device_id=(col, lax.rem(par + d, npar)), device_id_type=MESH,
        )

    for d in range(1, npar):
        cpart_copy(d).start()

    for d in range(1, npar):
        cpart_copy(d).wait()
    c_total = cpart_in[0]
    for q in range(1, npar):
        c_total = c_total + cpart_in[q]
    sums = [lane_sums(part[1 + g]) for g in range(2)]
    result = jnp.where(row == 0, sums[0], jnp.where(row == 1, sums[1], c_total))
    tot_out[...] = result
    tot_in[col] = result
    totals = []
    for d in range(1, ncol):
        copy = pltpu.make_async_remote_copy(
            src_ref=tot_out, dst_ref=tot_in.at[col],
            send_sem=t_ssem.at[d - 1], recv_sem=t_rsem.at[d - 1],
            device_id=(lax.rem(col + d, ncol), par), device_id_type=MESH,
        )
        copy.start()
        totals.append(copy)
    for d in range(1, npar):
        conc_copies[d - 1].wait_send()

    @pl.when(has_right)
    def _():
        wind_copy(0).wait_send()

    @pl.when(has_left)
    def _():
        wind_copy(1).wait_send()

    @pl.loop(0, chunks)
    def _(n):
        pair_copy(n, odd).wait_send()

        @pl.when(forwards)
        def _():
            forward_copy(n).wait_send()

    for copy in totals:
        copy.wait()
    total = tot_in[0]
    for q in range(1, ncol):
        total = total + tot_in[q]
    total = total / total_cells
    burd_ref[...] = total


def shards(
    concentration, emissions, rate_table, species_order, sensitivity, source_terms,
    courant_x, upwind_x, courant_y, upwind_y,
):
    ncol, npar = (lax.axis_size("cols"), lax.axis_size("params"))
    blocks, width = (rate_table.shape[0], rate_table.shape[1])
    groups, species, planes, layers, across = sensitivity.shape
    tall = planes * layers
    assert ncol % 2 == 0 and groups == 2 and tall == SUB and planes == 2 and across == 128
    cells = tall * across

    vm = pltpu.VMEM
    dma = pltpu.SemaphoreType.DMA
    rows_shape = (species * SUB, 128)
    in_vmem = pl.BlockSpec(memory_space=pltpu.VMEM)
    in_smem = pl.BlockSpec(memory_space=pltpu.SMEM)
    limits = pltpu.CompilerParams(vmem_limit_bytes=16 * 1024 * 1024)
    stacked = (groups, species, SUB, across)
    chunks = blocks * PARTS
    packed_shape = (chunks, width // PARTS, 2 * SUB, 128)
    newc_o, news_o, burd_o, order_o = pl.pallas_call(
        functools.partial(step_kernel, ncol, npar, blocks, width, cells * ncol),
        out_shape=(
            jax.ShapeDtypeStruct(rows_shape, jnp.float32),
            jax.ShapeDtypeStruct((groups * species * SUB, 128), jnp.float32),
            jax.ShapeDtypeStruct((SUB, species), jnp.float32),
            jax.ShapeDtypeStruct((1, species), jnp.int32),
        ),
        in_specs=[pl.BlockSpec(memory_space=pltpu.HBM)] * 10,
        out_specs=[in_vmem] * 4,
        scratch_shapes=[
            pltpu.SMEM((1, species), jnp.int32),
            pltpu.SMEM(rate_table.shape, jnp.float32),
            vm(concentration.shape, jnp.float32),
            vm(concentration.shape, jnp.float32),
            vm(stacked, jnp.float32),
            vm(stacked, jnp.bfloat16),
            vm((SUB, 128), jnp.float32),
            vm((SUB, 128), jnp.int32),
            vm((SUB, 128), jnp.float32),
            vm((SUB, 128), jnp.int32),
            vm((npar - 1,) + concentration.shape, jnp.float32),
            vm((species, SUB, 128), jnp.float32),
            vm((species, SUB, 128), jnp.float32),
            vm((blocks, width, SUB, 128), jnp.float32),
            vm((blocks, width, width, SUB, 128), jnp.float32),
            vm((10, SUB, 128), jnp.float32),
            vm((2, SUB, 128), jnp.float32),
            vm((2, 2, SUB, 128), jnp.float32),
            vm(packed_shape, jnp.bfloat16),
            vm((2,) + packed_shape, jnp.bfloat16),
            vm((3, species, 128), jnp.float32),
            vm((SUB, species), jnp.float32),
            vm((npar, SUB, species), jnp.float32),
            vm((SUB, species), jnp.float32),
            vm((ncol, SUB, species), jnp.float32),
            dma((11,)),
            dma((npar - 1,)), dma((npar - 1,)),
            dma((2,)), dma((2,)),
            dma((chunks,)), dma((chunks,)),
            dma((chunks,)), dma((chunks,)),
            dma((npar - 1,)), dma((npar - 1,)),
            dma((ncol - 1,)), dma((ncol - 1,)),
        ],
        compiler_params=pltpu.CompilerParams(
            collective_id=0, has_side_effects=True, vmem_limit_bytes=48 * 1024 * 1024
        ),
    )(
        pinned(species_order.reshape(1, species)), pinned(rate_table), pinned(concentration), pinned(emissions),
        pinned(sensitivity.reshape(stacked)), pinned(source_terms.reshape(stacked)),
        pinned(courant_x.reshape(SUB, across)), pinned(upwind_x.reshape(SUB, across)),
        pinned(courant_y.reshape(SUB, across)), pinned(upwind_y.reshape(SUB, across)),
    )
    newc, news, sburd, cburd = pl.pallas_call(
        restore_kernel,
        out_shape=(
            jax.ShapeDtypeStruct(concentration.shape, jnp.float32),
            jax.ShapeDtypeStruct(stacked, jnp.float32),
            jax.ShapeDtypeStruct((groups, species), jnp.float32),
            jax.ShapeDtypeStruct((1, species), jnp.float32),
        ),
        in_specs=[in_smem] + [in_vmem] * 4,
        out_specs=[pl.BlockSpec(memory_space=pltpu.HBM)] * 2 + [in_vmem] * 2,
        scratch_shapes=[
            vm(stacked, jnp.float32),
            vm((species, SUB, 128), jnp.float32),
            vm(concentration.shape, jnp.float32),
            dma((3,)),
        ],
        compiler_params=limits,
    )(order_o, order_o, newc_o.reshape((species, SUB, 128)), news_o.reshape(stacked), burd_o)
    return (newc, news.reshape(sensitivity.shape), sburd, cburd.reshape(species))


def solution(mesh):
    in_specs = (
        P(None, ("cols", "params")),
        P(None, ("cols", "params")),
        P(),
        P(),
        P("params", None, "cols", None, None),
        P("params", None, "cols", None, None),
        P("cols", None, None),
        P("cols", None, None),
        P("cols", None, None),
        P("cols", None, None),
    )
    out_specs = (
        P(None, ("cols", "params")),
        P("params", None, "cols", None, None),
        P("params", None),
        P(),
    )
    return jax.shard_map(shards, mesh=mesh, in_specs=in_specs, out_specs=out_specs, check_vma=False)
```

```python
import functools
import jax
import jax.numpy as jnp
from jax import lax
from jax.experimental import pallas as pl
from jax.experimental.pallas import tpu as pltpu
from jax.sharding import PartitionSpec as P

MESH = pl.DeviceIdType.MESH
SUB = 8
PARTS = 2
LAG = 3


def pinned(value):
    return pltpu.with_memory_space_constraint(value, pltpu.HBM)


def restore_kernel(order, order_row, newc_o, news_o, burd_o, newc_hbm, news_hbm, sburd_hbm, cburd_hbm, news_ref, newc_rows, newc_ref, sburd, cburd, sems):
    species = news_o.shape[1]
    rows = newc_ref.shape[1] // 128
    first = lax.axis_index("params") * rows

    def put(group):
        @pl.loop(0, species, unroll=32)
        def _(k):
            news_ref[group, order[0, k]] = news_o[group, k]

        copy = pltpu.make_async_copy(news_ref.at[group], news_hbm.at[group], sems.at[group])
        copy.start()
        return copy

    copies = [put(0), put(1)]

    @pl.loop(0, species, unroll=32)
    def _(k):
        newc_rows[order[0, k]] = newc_o[k]

    flat = newc_rows.reshape(species * SUB, 128)
    for t in range(species // SUB):
        for r in range(rows):
            newc_ref[t * SUB:(t + 1) * SUB, r * 128:(r + 1) * 128] = flat[pl.ds(t * SUB * SUB + first + r, SUB, stride=SUB), :]
    copies.append(pltpu.make_async_copy(newc_ref, newc_hbm, sems.at[2]))
    copies[2].start()
    at = lax.broadcasted_iota(jnp.int32, (species, species), 0)
    turn = jnp.where(at == order_row[...], 1.0, 0.0).astype(jnp.float32)
    total = lax.dot_general(
        burd_o[...], turn, (((1,), (1,)), ((), ())),
        precision=lax.Precision.HIGHEST, preferred_element_type=jnp.float32,
    )
    sburd[...] = total[:2]
    cburd[...] = total[2:3]
    copies.append(pltpu.make_async_copy(sburd, sburd_hbm, sems.at[3]))
    copies.append(pltpu.make_async_copy(cburd, cburd_hbm, sems.at[4]))
    for copy in copies[3:]:
        copy.start()
    for copy in copies:
        copy.wait()


def step_kernel(
    ncol, npar, blocks, width, total_cells,
    order_hbm, rate_hbm, conc_hbm, emis_hbm, sens_hbm, src_hbm, cx_hbm, ux_hbm, cy_hbm, uy_hbm,
    newc_ref, news_ref, burd_ref, order_out,
    order, rate, conc_ref, emis_ref, sens_ref, src_ref, cx_ref, ux_ref, cy_ref, uy_ref,
    conc_in, conc_rows, emis_rows, invc, lu, coef, wind, wind_in,
    send, halo, part, cpart, cpart_in, tot_out, tot_in,
    in_sem, conc_ssem, conc_rsem, w_ssem, w_rsem, p_ssem, p_rsem, f_ssem, f_rsem, cp_ssem, cp_rsem, t_ssem, t_rsem,
):
    species = blocks * width
    part_width = width // PARTS
    chunks = blocks * PARTS
    half = SUB // 2
    col, par = (lax.axis_index("cols"), lax.axis_index("params"))
    rows = conc_ref.shape[1] // 128
    has_left, has_right = (col > 0, col < ncol - 1)
    odd = lax.rem(col, 2)
    other = 1 - odd
    partner = col + 1 - 2 * odd
    ahead = col + 2 - 4 * odd
    forwards = jnp.logical_and(ahead >= 0, ahead < ncol)
    ahead = jnp.clip(ahead, 0, ncol - 1)
    behind = col - 2 + 4 * odd
    receives = jnp.logical_and(behind >= 0, behind < ncol)

    barrier = pltpu.get_barrier_semaphore()
    for d in range(1, ncol):
        pl.semaphore_signal(barrier, inc=1, device_id=(lax.rem(col + d, ncol), par), device_id_type=MESH)
    for d in range(1, npar):
        pl.semaphore_signal(barrier, inc=1, device_id=(col, lax.rem(par + d, npar)), device_id_type=MESH)

    held = (
        (order_hbm, order), (sens_hbm, sens_ref), (cx_hbm, cx_ref), (ux_hbm, ux_ref), (cy_hbm, cy_ref), (uy_hbm, uy_ref),
        (conc_hbm, conc_ref), (emis_hbm, emis_ref), (rate_hbm, rate), (src_hbm, src_ref), (order_hbm, order_out),
    )
    loads = [pltpu.make_async_copy(src, dst, in_sem.at[n]) for n, (src, dst) in enumerate(held)]
    for load in loads:
        load.start()

    row = lax.broadcasted_iota(jnp.int32, (SUB, 128), 0)
    lane = lax.broadcasted_iota(jnp.int32, (SUB, 128), 1)
    top = row < half

    @pl.when(jnp.logical_not(has_left))
    def _():
        halo[0] = jnp.zeros_like(halo[0])
        wind_in[0] = jnp.zeros_like(wind_in[0])

    @pl.when(jnp.logical_not(has_right))
    def _():
        halo[1] = jnp.zeros_like(halo[1])
        wind_in[1] = jnp.zeros_like(wind_in[1])

    def wind_copy(way):
        target = jnp.minimum(col + 1, ncol - 1) if way == 0 else jnp.maximum(col - 1, 0)
        return pltpu.make_async_remote_copy(
            src_ref=wind, dst_ref=wind_in.at[way], send_sem=w_ssem.at[way], recv_sem=w_rsem.at[way],
            device_id=(target, par), device_id_type=MESH,
        )

    def pair_copy(n, side):
        return pltpu.make_async_remote_copy(
            src_ref=send.at[n], dst_ref=halo.at[side, n], send_sem=p_ssem.at[n], recv_sem=p_rsem.at[n],
            device_id=(partner, par), device_id_type=MESH,
        )

    def forward_copy(n):
        return pltpu.make_async_remote_copy(
            src_ref=halo.at[other, n], dst_ref=halo.at[odd, n], send_sem=f_ssem.at[n], recv_sem=f_rsem.at[n],
            device_id=(ahead, par), device_id_type=MESH,
        )

    def pass_on(n):
        pair_copy(n, other).wait_recv()

        @pl.when(forwards)
        def _():
            forward_copy(n).start()

    def pack(n):
        for k in range(part_width):
            at = order[0, n * part_width + k]
            both = jnp.concatenate([sens_ref[0, at], sens_ref[1, at]], axis=0)
            send[n, k] = both.astype(jnp.bfloat16)

    for load in loads[2:6]:
        load.wait()
    wind[0] = jnp.where(ux_ref[...] == 1, cx_ref[...], -cx_ref[...])
    wind[1] = jnp.where(uy_ref[...] == 1, cy_ref[...], -cy_ref[...])
    loads[6].wait()
    loads[0].wait()
    loads[1].wait()
    pack(0)
    pl.semaphore_wait(barrier, ncol - 1 + npar - 1)
    conc_copies = []
    for d in range(1, npar):
        copy = pltpu.make_async_remote_copy(
            src_ref=conc_ref, dst_ref=conc_in.at[npar - 1 - d],
            send_sem=conc_ssem.at[d - 1], recv_sem=conc_rsem.at[npar - 1 - d],
            device_id=(col, lax.rem(par + d, npar)), device_id_type=MESH,
        )
        copy.start()
        conc_copies.append(copy)
    pair_copy(0, odd).start()

    @pl.when(has_right)
    def _():
        wind_copy(0).start()

    @pl.when(has_left)
    def _():
        wind_copy(1).start()

    @pl.loop(1, chunks)
    def _(n):
        pack(n)
        pair_copy(n, odd).start()

    def spread(read, target, base):
        target = target.reshape(species * SUB, 128)

        @pl.loop(0, species // SUB)
        def _(t):
            for r in range(rows):
                target[pl.ds(t * SUB * SUB + base + r, SUB, stride=SUB), :] = read(t, r)

    def own(ref):
        return lambda t, r: ref[pl.ds(pl.multiple_of(t * SUB, SUB), SUB), r * 128:(r + 1) * 128]

    spread(own(conc_ref), conc_rows, par * rows)
    loads[7].wait()
    spread(own(emis_ref), emis_rows, par * rows)
    for load in loads[8:]:
        load.wait()

    def set_coefficients():
        @pl.when(has_left)
        def _():
            wind_copy(0).wait_recv()

        @pl.when(has_right)
        def _():
            wind_copy(1).wait_recv()

        zero = jnp.zeros((SUB, 128), jnp.float32)

        def split(value):
            return (jnp.maximum(value, zero), jnp.maximum(-value, zero))

        def swap(value):
            return pltpu.roll(value, half, 0)

        def across(value):
            into, out = split(value)
            last = lane == 127
            next_in = jnp.where(last, zero, pltpu.roll(into, 127, 1))
            next_out = jnp.where(last, zero, pltpu.roll(out, 127, 1))
            return (out + next_in, jnp.where(lane == 0, zero, into), next_out)

        own_x, left_x, right_x = (wind[0], wind_in[0, 0], wind_in[1, 0])
        in_x, out_x = split(own_x)
        next_in, next_out = split(jnp.where(top, swap(own_x), swap(right_x)))
        lost, down, up = across(wind[1])
        coef[0] = 1.0 - (out_x + next_in) - lost
        coef[1] = jnp.where(jnp.logical_and(top, jnp.logical_not(has_left)), zero, in_x)
        coef[2] = next_out
        coef[3] = down
        coef[4] = up
        in_x, out_x = split(jnp.where(top, swap(left_x), swap(right_x)))
        next_in, next_out = split(jnp.where(top, own_x, right_x))
        lost, down, up = across(jnp.where(top, swap(wind_in[0, 1]), swap(wind_in[1, 1])))
        coef[5] = 1.0 - (out_x + next_in) - lost
        coef[6] = in_x
        coef[7] = next_out
        coef[8] = down
        coef[9] = up

    def stencil(first, value, before, after):
        a0, al, ar, ad, au = (coef[first + n] for n in range(5))
        return (
            a0 * value + al * before + ar * after
            + ad * pltpu.roll(value, 1, 1) + au * pltpu.roll(value, 127, 1)
        )

    def advance(s, h):
        turned = pltpu.roll(s, half, 0)
        return stencil(0, s, jnp.where(top, h, turned), jnp.where(top, turned, h))

    def transport(s, left, right):
        h = pltpu.roll(jnp.where(top, right, left), half, 0)
        next_h = stencil(5, h, jnp.where(top, left, s), jnp.where(top, s, right))
        return advance(advance(s, h), next_h)

    for d in range(1, npar):
        conc_copies[npar - 1 - d].wait_recv()
        spread(own(conc_in.at[d - 1]), conc_rows, lax.rem(par + d, npar) * rows)

    set_coefficients()

    def factorize(b):
        c = [conc_rows[order[0, b * width + j]] for j in range(width)]
        for i in range(width):
            invc[b, i] = 1.0 / c[i]

        def fresh(i):
            rates = [rate[b, i, j] for j in range(width)]
            total = rates[0] * c[0]
            for j in range(1, width):
                total = total + rates[j] * c[j]
            diagonal = (1.0 + total) * invc[b, i] - rates[i]
            return [diagonal if j == i else jnp.full((SUB, 128), -rates[j], jnp.float32) for j in range(width)]

        for i in range(0, width, 2):
            x, y = (fresh(i), fresh(i + 1))
            for k in range(i):
                inv = lu[b, k, k]
                lx, ly = (x[k] * inv, y[k] * inv)
                lu[b, i, k] = lx
                lu[b, i + 1, k] = ly
                for j in range(k + 1, width):
                    u = lu[b, k, j]
                    x[j] = x[j] - lx * u
                    y[j] = y[j] - ly * u
            inv = 1.0 / x[i]
            lu[b, i, i] = inv
            ly = y[i] * inv
            lu[b, i + 1, i] = ly
            for j in range(i + 1, width):
                lu[b, i, j] = x[j]
                y[j] = y[j] - ly * x[j]
            lu[b, i + 1, i + 1] = 1.0 / y[i + 1]
            for j in range(i + 2, width):
                lu[b, i + 1, j] = y[j]

    def solve(b, sides):
        sides = [list(side) for side in sides]
        for k in range(width):
            for i in range(k + 1, width):
                low = lu[b, i, k]
                for side in sides:
                    side[i] = side[i] - low * side[k]
        for k in range(width - 1, -1, -1):
            inv = lu[b, k, k]
            for side in sides:
                side[k] = side[k] * inv
            for i in range(k):
                up = lu[b, i, k]
                for side in sides:
                    side[i] = side[i] - up * side[k]
        return [[side[k] * invc[b, k] for k in range(width)] for side in sides]

    def first_half(b):
        factorize(b)
        base = []
        for k in range(width):
            at = order[0, b * width + k]
            base.append(conc_rows[at] + emis_rows[at])
        (base,) = solve(b, [base])
        for k in range(width):
            o = b * width + k
            newc_ref[pl.ds(pl.multiple_of(o * SUB, SUB), SUB), :] = base[k]

    def second_half(b):
        sides = [[], []]
        for k in range(width):
            at = order[0, b * width + k]
            n, m = (b * PARTS + k // part_width, k % part_width)
            left, right = (halo[0, n, m].astype(jnp.float32), halo[1, n, m].astype(jnp.float32))
            for g in range(2):
                rows_g = slice(g * SUB, (g + 1) * SUB)
                moved = transport(sens_ref[g, at], left[rows_g], right[rows_g])
                sides[g].append(moved + src_ref[g, at].astype(jnp.float32))
        sides = solve(b, sides)
        for g in range(2):
            for k in range(width):
                at = (g * species + b * width + k) * SUB
                news_ref[pl.ds(pl.multiple_of(at, SUB), SUB), :] = sides[g][k]
        for g in range(2):
            for t in range(width // SUB):
                first = b * width + t * SUB
                total = jnp.zeros((SUB, 128), jnp.float32)
                for r in range(SUB):
                    total = total + news_ref[pl.ds((g * species + first) * SUB + r, SUB, stride=SUB), :]
                part[1 + g, pl.ds(pl.multiple_of(first, SUB), SUB), :] = total

    ones = jnp.ones((SUB, 128), jnp.bfloat16)

    def lane_sums(value):
        high = value.astype(jnp.bfloat16)
        low = (value - high.astype(jnp.float32)).astype(jnp.bfloat16)
        both = [
            lax.dot_general(ones, piece, (((1,), (1,)), ((), ())), preferred_element_type=jnp.float32)
            for piece in (high, low)
        ]
        return both[0] + both[1]

    def cpart_copy(d):
        return pltpu.make_async_remote_copy(
            src_ref=cpart, dst_ref=cpart_in.at[par],
            send_sem=cp_ssem.at[d - 1], recv_sem=cp_rsem.at[d - 1],
            device_id=(col, lax.rem(par + d, npar)), device_id_type=MESH,
        )

    def close_base():
        @pl.loop(0, species // SUB)
        def _(t):
            total = jnp.zeros((SUB, 128), jnp.float32)
            at = pl.ds(pl.multiple_of(t * SUB, SUB), SUB)
            for r in range(rows):
                total = total + newc_ref[pl.ds(t * SUB * SUB + par * rows + r, SUB, stride=SUB), :]
            part[0, at, :] = total

        own_c = lane_sums(part[0])
        cpart[...] = own_c
        cpart_in[par] = own_c

        for d in range(1, npar):
            cpart_copy(d).start()

    @pl.loop(0, blocks + LAG)
    def _(step):
        @pl.when(step < blocks)
        def _():
            for n in range(PARTS // 2):
                pass_on(step * PARTS + n)
            first_half(step)
            for n in range(PARTS // 2, PARTS):
                pass_on(step * PARTS + n)

        @pl.when(step == blocks - 1)
        def _():
            close_base()

        @pl.when(step >= LAG)
        def _():
            b = step - LAG

            @pl.when(receives)
            def _():
                for n in range(PARTS):
                    forward_copy(b * PARTS + n).wait_recv()

            second_half(b)

    for d in range(1, npar):
        cpart_copy(d).wait()
    c_total = cpart_in[0]
    for q in range(1, npar):
        c_total = c_total + cpart_in[q]
    sums = [lane_sums(part[1 + g]) for g in range(2)]
    result = jnp.where(row == 0, sums[0], jnp.where(row == 1, sums[1], c_total))
    tot_out[...] = result
    tot_in[col] = result
    totals = []
    for d in range(1, ncol):
        copy = pltpu.make_async_remote_copy(
            src_ref=tot_out, dst_ref=tot_in.at[col],
            send_sem=t_ssem.at[d - 1], recv_sem=t_rsem.at[d - 1],
            device_id=(lax.rem(col + d, ncol), par), device_id_type=MESH,
        )
        copy.start()
        totals.append(copy)
    for d in range(1, npar):
        conc_copies[d - 1].wait_send()

    @pl.when(has_right)
    def _():
        wind_copy(0).wait_send()

    @pl.when(has_left)
    def _():
        wind_copy(1).wait_send()

    @pl.loop(0, chunks)
    def _(n):
        pair_copy(n, odd).wait_send()

        @pl.when(forwards)
        def _():
            forward_copy(n).wait_send()

    for copy in totals:
        copy.wait()
    total = tot_in[0]
    for q in range(1, ncol):
        total = total + tot_in[q]
    total = total / total_cells
    burd_ref[...] = total


def shards(
    concentration, emissions, rate_table, species_order, sensitivity, source_terms,
    courant_x, upwind_x, courant_y, upwind_y,
):
    ncol, npar = (lax.axis_size("cols"), lax.axis_size("params"))
    blocks, width = (rate_table.shape[0], rate_table.shape[1])
    groups, species, planes, layers, across = sensitivity.shape
    tall = planes * layers
    assert ncol % 2 == 0 and groups == 2 and tall == SUB and planes == 2 and across == 128
    cells = tall * across

    vm = pltpu.VMEM
    dma = pltpu.SemaphoreType.DMA
    rows_shape = (species * SUB, 128)
    in_vmem = pl.BlockSpec(memory_space=pltpu.VMEM)
    in_smem = pl.BlockSpec(memory_space=pltpu.SMEM)
    limits = pltpu.CompilerParams(vmem_limit_bytes=16 * 1024 * 1024)
    stacked = (groups, species, SUB, across)
    chunks = blocks * PARTS
    packed_shape = (chunks, width // PARTS, 2 * SUB, 128)
    newc_o, news_o, burd_o, order_o = pl.pallas_call(
        functools.partial(step_kernel, ncol, npar, blocks, width, cells * ncol),
        out_shape=(
            jax.ShapeDtypeStruct(rows_shape, jnp.float32),
            jax.ShapeDtypeStruct((groups * species * SUB, 128), jnp.float32),
            jax.ShapeDtypeStruct((SUB, species), jnp.float32),
            jax.ShapeDtypeStruct((1, species), jnp.int32),
        ),
        in_specs=[pl.BlockSpec(memory_space=pltpu.HBM)] * 10,
        out_specs=[in_vmem] * 4,
        scratch_shapes=[
            pltpu.SMEM((1, species), jnp.int32),
            pltpu.SMEM(rate_table.shape, jnp.float32),
            vm(concentration.shape, jnp.float32),
            vm(concentration.shape, jnp.float32),
            vm(stacked, jnp.float32),
            vm(stacked, jnp.bfloat16),
            vm((SUB, 128), jnp.float32),
            vm((SUB, 128), jnp.int32),
            vm((SUB, 128), jnp.float32),
            vm((SUB, 128), jnp.int32),
            vm((npar - 1,) + concentration.shape, jnp.float32),
            vm((species, SUB, 128), jnp.float32),
            vm((species, SUB, 128), jnp.float32),
            vm((blocks, width, SUB, 128), jnp.float32),
            vm((blocks, width, width, SUB, 128), jnp.float32),
            vm((10, SUB, 128), jnp.float32),
            vm((2, SUB, 128), jnp.float32),
            vm((2, 2, SUB, 128), jnp.float32),
            vm(packed_shape, jnp.bfloat16),
            vm((2,) + packed_shape, jnp.bfloat16),
            vm((3, species, 128), jnp.float32),
            vm((SUB, species), jnp.float32),
            vm((npar, SUB, species), jnp.float32),
            vm((SUB, species), jnp.float32),
            vm((ncol, SUB, species), jnp.float32),
            dma((11,)),
            dma((npar - 1,)), dma((npar - 1,)),
            dma((2,)), dma((2,)),
            dma((chunks,)), dma((chunks,)),
            dma((chunks,)), dma((chunks,)),
            dma((npar - 1,)), dma((npar - 1,)),
            dma((ncol - 1,)), dma((ncol - 1,)),
        ],
        compiler_params=pltpu.CompilerParams(
            collective_id=0, has_side_effects=True, vmem_limit_bytes=48 * 1024 * 1024
        ),
    )(
        pinned(species_order.reshape(1, species)), pinned(rate_table), pinned(concentration), pinned(emissions),
        pinned(sensitivity.reshape(stacked)), pinned(source_terms.reshape(stacked)),
        pinned(courant_x.reshape(SUB, across)), pinned(upwind_x.reshape(SUB, across)),
        pinned(courant_y.reshape(SUB, across)), pinned(upwind_y.reshape(SUB, across)),
    )
    newc, news, sburd, cburd = pl.pallas_call(
        restore_kernel,
        out_shape=(
            jax.ShapeDtypeStruct(concentration.shape, jnp.float32),
            jax.ShapeDtypeStruct(stacked, jnp.float32),
            jax.ShapeDtypeStruct((groups, species), jnp.float32),
            jax.ShapeDtypeStruct((1, species), jnp.float32),
        ),
        in_specs=[in_smem] + [in_vmem] * 4,
        out_specs=[pl.BlockSpec(memory_space=pltpu.HBM)] * 4,
        scratch_shapes=[
            vm(stacked, jnp.float32),
            vm((species, SUB, 128), jnp.float32),
            vm(concentration.shape, jnp.float32),
            vm((groups, species), jnp.float32),
            vm((1, species), jnp.float32),
            dma((5,)),
        ],
        compiler_params=limits,
    )(order_o, order_o, newc_o.reshape((species, SUB, 128)), news_o.reshape(stacked), burd_o)
    return (newc, news.reshape(sensitivity.shape), sburd, cburd.reshape(species))


def solution(mesh):
    in_specs = (
        P(None, ("cols", "params")),
        P(None, ("cols", "params")),
        P(),
        P(),
        P("params", None, "cols", None, None),
        P("params", None, "cols", None, None),
        P("cols", None, None),
        P("cols", None, None),
        P("cols", None, None),
        P("cols", None, None),
    )
    out_specs = (
        P(None, ("cols", "params")),
        P("params", None, "cols", None, None),
        P("params", None),
        P(),
    )
    return jax.shard_map(shards, mesh=mesh, in_specs=in_specs, out_specs=out_specs, check_vma=False)
```

```python
import functools
import jax
import jax.numpy as jnp
from jax import lax
from jax.experimental import pallas as pl
from jax.experimental.pallas import tpu as pltpu
from jax.sharding import PartitionSpec as P

MESH = pl.DeviceIdType.MESH
SUB = 8
PARTS = 2
LAG = 3


def pinned(value):
    return pltpu.with_memory_space_constraint(value, pltpu.HBM)


def write_kernel(order_row, newc_o, news_o, burd_o, newc_hbm, news_hbm, sburd_hbm, cburd_hbm, sburd, cburd, sems):
    species = newc_o.shape[0]
    held = ((news_o, news_hbm), (newc_o, newc_hbm), (sburd, sburd_hbm), (cburd, cburd_hbm))
    copies = [pltpu.make_async_copy(src, dst, sems.at[n]) for n, (src, dst) in enumerate(held)]
    for copy in copies[:2]:
        copy.start()
    at = lax.broadcasted_iota(jnp.int32, (species, species), 0)
    turn = jnp.where(at == order_row[...], 1.0, 0.0).astype(jnp.float32)
    total = lax.dot_general(
        burd_o[...], turn, (((1,), (1,)), ((), ())),
        precision=lax.Precision.HIGHEST, preferred_element_type=jnp.float32,
    )
    sburd[...] = total[:2]
    cburd[...] = total[2:3]
    for copy in copies[2:]:
        copy.start()
    for copy in copies:
        copy.wait()


def step_kernel(
    ncol, npar, blocks, width, total_cells,
    order_hbm, rate_hbm, conc_hbm, emis_hbm, sens_hbm, src_hbm, cx_hbm, ux_hbm, cy_hbm, uy_hbm,
    newc_ref, news_ref, burd_ref, order_out,
    order, rate, conc_ref, emis_ref, sens_ref, src_ref, cx_ref, ux_ref, cy_ref, uy_ref,
    place, place_row, conc_in, conc_rows, emis_rows, newc_rows, news_rows, invc, lu, coef, wind, wind_in,
    send, halo, part, cpart, cpart_in, tot_out, tot_in,
    in_sem, place_sem, conc_ssem, conc_rsem, w_ssem, w_rsem, p_ssem, p_rsem, f_ssem, f_rsem, cp_ssem, cp_rsem, t_ssem, t_rsem,
):
    species = blocks * width
    part_width = width // PARTS
    chunks = blocks * PARTS
    half = SUB // 2
    col, par = (lax.axis_index("cols"), lax.axis_index("params"))
    rows = conc_ref.shape[1] // 128
    has_left, has_right = (col > 0, col < ncol - 1)
    odd = lax.rem(col, 2)
    other = 1 - odd
    partner = col + 1 - 2 * odd
    ahead = col + 2 - 4 * odd
    forwards = jnp.logical_and(ahead >= 0, ahead < ncol)
    ahead = jnp.clip(ahead, 0, ncol - 1)
    behind = col - 2 + 4 * odd
    receives = jnp.logical_and(behind >= 0, behind < ncol)

    barrier = pltpu.get_barrier_semaphore()
    for d in range(1, ncol):
        pl.semaphore_signal(barrier, inc=1, device_id=(lax.rem(col + d, ncol), par), device_id_type=MESH)
    for d in range(1, npar):
        pl.semaphore_signal(barrier, inc=1, device_id=(col, lax.rem(par + d, npar)), device_id_type=MESH)

    held = (
        (order_hbm, order), (sens_hbm, sens_ref), (cx_hbm, cx_ref), (ux_hbm, ux_ref), (cy_hbm, cy_ref), (uy_hbm, uy_ref),
        (conc_hbm, conc_ref), (emis_hbm, emis_ref), (rate_hbm, rate), (src_hbm, src_ref), (order_hbm, order_out),
    )
    loads = [pltpu.make_async_copy(src, dst, in_sem.at[n]) for n, (src, dst) in enumerate(held)]
    for load in loads:
        load.start()

    row = lax.broadcasted_iota(jnp.int32, (SUB, 128), 0)
    lane = lax.broadcasted_iota(jnp.int32, (SUB, 128), 1)
    top = row < half

    @pl.when(jnp.logical_not(has_left))
    def _():
        halo[0] = jnp.zeros_like(halo[0])
        wind_in[0] = jnp.zeros_like(wind_in[0])

    @pl.when(jnp.logical_not(has_right))
    def _():
        halo[1] = jnp.zeros_like(halo[1])
        wind_in[1] = jnp.zeros_like(wind_in[1])

    def wind_copy(way):
        target = jnp.minimum(col + 1, ncol - 1) if way == 0 else jnp.maximum(col - 1, 0)
        return pltpu.make_async_remote_copy(
            src_ref=wind, dst_ref=wind_in.at[way], send_sem=w_ssem.at[way], recv_sem=w_rsem.at[way],
            device_id=(target, par), device_id_type=MESH,
        )

    def pair_copy(n, side):
        return pltpu.make_async_remote_copy(
            src_ref=send.at[n], dst_ref=halo.at[side, n], send_sem=p_ssem.at[n], recv_sem=p_rsem.at[n],
            device_id=(partner, par), device_id_type=MESH,
        )

    def forward_copy(n):
        return pltpu.make_async_remote_copy(
            src_ref=halo.at[other, n], dst_ref=halo.at[odd, n], send_sem=f_ssem.at[n], recv_sem=f_rsem.at[n],
            device_id=(ahead, par), device_id_type=MESH,
        )

    def pass_on(n):
        pair_copy(n, other).wait_recv()

        @pl.when(forwards)
        def _():
            forward_copy(n).start()

    def pack(n):
        for k in range(part_width):
            at = order[0, n * part_width + k]
            both = jnp.concatenate([sens_ref[0, at], sens_ref[1, at]], axis=0)
            send[n, k] = both.astype(jnp.bfloat16)

    for load in loads[2:6]:
        load.wait()
    wind[0] = jnp.where(ux_ref[...] == 1, cx_ref[...], -cx_ref[...])
    wind[1] = jnp.where(uy_ref[...] == 1, cy_ref[...], -cy_ref[...])
    loads[6].wait()
    loads[0].wait()
    loads[1].wait()
    pack(0)
    pl.semaphore_wait(barrier, ncol - 1 + npar - 1)
    conc_copies = []
    for d in range(1, npar):
        copy = pltpu.make_async_remote_copy(
            src_ref=conc_ref, dst_ref=conc_in.at[npar - 1 - d],
            send_sem=conc_ssem.at[d - 1], recv_sem=conc_rsem.at[npar - 1 - d],
            device_id=(col, lax.rem(par + d, npar)), device_id_type=MESH,
        )
        copy.start()
        conc_copies.append(copy)
    pair_copy(0, odd).start()

    @pl.when(has_right)
    def _():
        wind_copy(0).start()

    @pl.when(has_left)
    def _():
        wind_copy(1).start()

    @pl.loop(1, chunks)
    def _(n):
        pack(n)
        pair_copy(n, odd).start()

    def spread(read, target, base):
        target = target.reshape(species * SUB, 128)

        @pl.loop(0, species // SUB)
        def _(t):
            for r in range(rows):
                target[pl.ds(t * SUB * SUB + base + r, SUB, stride=SUB), :] = read(t, r)

    def own(ref):
        return lambda t, r: ref[pl.ds(pl.multiple_of(t * SUB, SUB), SUB), r * 128:(r + 1) * 128]

    spread(own(conc_ref), conc_rows, par * rows)
    loads[7].wait()
    spread(own(emis_ref), emis_rows, par * rows)
    for load in loads[8:]:
        load.wait()

    def set_coefficients():
        @pl.when(has_left)
        def _():
            wind_copy(0).wait_recv()

        @pl.when(has_right)
        def _():
            wind_copy(1).wait_recv()

        zero = jnp.zeros((SUB, 128), jnp.float32)

        def split(value):
            return (jnp.maximum(value, zero), jnp.maximum(-value, zero))

        def swap(value):
            return pltpu.roll(value, half, 0)

        def across(value):
            into, out = split(value)
            last = lane == 127
            next_in = jnp.where(last, zero, pltpu.roll(into, 127, 1))
            next_out = jnp.where(last, zero, pltpu.roll(out, 127, 1))
            return (out + next_in, jnp.where(lane == 0, zero, into), next_out)

        own_x, left_x, right_x = (wind[0], wind_in[0, 0], wind_in[1, 0])
        in_x, out_x = split(own_x)
        next_in, next_out = split(jnp.where(top, swap(own_x), swap(right_x)))
        lost, down, up = across(wind[1])
        coef[0] = 1.0 - (out_x + next_in) - lost
        coef[1] = jnp.where(jnp.logical_and(top, jnp.logical_not(has_left)), zero, in_x)
        coef[2] = next_out
        coef[3] = down
        coef[4] = up
        in_x, out_x = split(jnp.where(top, swap(left_x), swap(right_x)))
        next_in, next_out = split(jnp.where(top, own_x, right_x))
        lost, down, up = across(jnp.where(top, swap(wind_in[0, 1]), swap(wind_in[1, 1])))
        coef[5] = 1.0 - (out_x + next_in) - lost
        coef[6] = in_x
        coef[7] = next_out
        coef[8] = down
        coef[9] = up

    def stencil(first, value, before, after):
        a0, al, ar, ad, au = (coef[first + n] for n in range(5))
        return (
            a0 * value + al * before + ar * after
            + ad * pltpu.roll(value, 1, 1) + au * pltpu.roll(value, 127, 1)
        )

    def advance(s, h):
        turned = pltpu.roll(s, half, 0)
        return stencil(0, s, jnp.where(top, h, turned), jnp.where(top, turned, h))

    def transport(s, left, right):
        h = pltpu.roll(jnp.where(top, right, left), half, 0)
        next_h = stencil(5, h, jnp.where(top, left, s), jnp.where(top, s, right))
        return advance(advance(s, h), next_h)

    pass_on(0)
    for d in range(1, npar):
        conc_copies[npar - 1 - d].wait_recv()
        spread(own(conc_in.at[d - 1]), conc_rows, lax.rem(par + d, npar) * rows)

    set_coefficients()

    def factorize(b):
        c = [conc_rows[order[0, b * width + j]] for j in range(width)]
        for i in range(width):
            invc[b, i] = 1.0 / c[i]

        def fresh(i):
            rates = [rate[b, i, j] for j in range(width)]
            total = rates[0] * c[0]
            for j in range(1, width):
                total = total + rates[j] * c[j]
            diagonal = (1.0 + total) * invc[b, i] - rates[i]
            return [diagonal if j == i else jnp.full((SUB, 128), -rates[j], jnp.float32) for j in range(width)]

        for i in range(0, width, 2):
            x, y = (fresh(i), fresh(i + 1))
            for k in range(i):
                inv = lu[b, k, k]
                lx, ly = (x[k] * inv, y[k] * inv)
                lu[b, i, k] = lx
                lu[b, i + 1, k] = ly
                for j in range(k + 1, width):
                    u = lu[b, k, j]
                    x[j] = x[j] - lx * u
                    y[j] = y[j] - ly * u
            inv = 1.0 / x[i]
            lu[b, i, i] = inv
            ly = y[i] * inv
            lu[b, i + 1, i] = ly
            for j in range(i + 1, width):
                lu[b, i, j] = x[j]
                y[j] = y[j] - ly * x[j]
            lu[b, i + 1, i + 1] = 1.0 / y[i + 1]
            for j in range(i + 2, width):
                lu[b, i + 1, j] = y[j]

    def solve(b, sides):
        sides = [list(side) for side in sides]
        for k in range(width):
            for i in range(k + 1, width):
                low = lu[b, i, k]
                for side in sides:
                    side[i] = side[i] - low * side[k]
        for k in range(width - 1, -1, -1):
            inv = lu[b, k, k]
            for side in sides:
                side[k] = side[k] * inv
            for i in range(k):
                up = lu[b, i, k]
                for side in sides:
                    side[i] = side[i] - up * side[k]
        return [[side[k] * invc[b, k] for k in range(width)] for side in sides]

    def first_half(b):
        factorize(b)
        base = []
        for k in range(width):
            at = order[0, b * width + k]
            base.append(conc_rows[at] + emis_rows[at])
        (base,) = solve(b, [base])
        for k in range(width):
            o = b * width + k
            newc_rows[o] = base[k]

    def second_half(b):
        sides = [[], []]
        for k in range(width):
            at = order[0, b * width + k]
            n, m = (b * PARTS + k // part_width, k % part_width)
            left, right = (halo[0, n, m].astype(jnp.float32), halo[1, n, m].astype(jnp.float32))
            for g in range(2):
                rows_g = slice(g * SUB, (g + 1) * SUB)
                moved = transport(sens_ref[g, at], left[rows_g], right[rows_g])
                sides[g].append(moved + src_ref[g, at].astype(jnp.float32))
        sides = solve(b, sides)
        for g in range(2):
            for k in range(width):
                news_rows[g, b * width + k] = sides[g][k]
        flat = news_rows.reshape(2 * species * SUB, 128)
        for g in range(2):
            for t in range(width // SUB):
                first = b * width + t * SUB
                total = jnp.zeros((SUB, 128), jnp.float32)
                for r in range(SUB):
                    total = total + flat[pl.ds((g * species + first) * SUB + r, SUB, stride=SUB), :]
                part[1 + g, pl.ds(pl.multiple_of(first, SUB), SUB), :] = total

    ones = jnp.ones((SUB, 128), jnp.bfloat16)

    def lane_sums(value):
        high = value.astype(jnp.bfloat16)
        low = (value - high.astype(jnp.float32)).astype(jnp.bfloat16)
        both = [
            lax.dot_general(ones, piece, (((1,), (1,)), ((), ())), preferred_element_type=jnp.float32)
            for piece in (high, low)
        ]
        return both[0] + both[1]

    def cpart_copy(d):
        return pltpu.make_async_remote_copy(
            src_ref=cpart, dst_ref=cpart_in.at[par],
            send_sem=cp_ssem.at[d - 1], recv_sem=cp_rsem.at[d - 1],
            device_id=(col, lax.rem(par + d, npar)), device_id_type=MESH,
        )

    def close_base():
        @pl.loop(0, species // SUB)
        def _(t):
            total = jnp.zeros((SUB, 128), jnp.float32)
            at = pl.ds(pl.multiple_of(t * SUB, SUB), SUB)
            for r in range(rows):
                total = total + newc_rows.reshape(species * SUB, 128)[pl.ds(t * SUB * SUB + par * rows + r, SUB, stride=SUB), :]
            part[0, at, :] = total

        own_c = lane_sums(part[0])
        cpart[...] = own_c
        cpart_in[par] = own_c

        for d in range(1, npar):
            cpart_copy(d).start()

    @pl.loop(0, blocks + LAG)
    def _(step):
        @pl.when(step < blocks)
        def _():
            first_half(step)
            pass_on(step * PARTS + 1)

        @pl.when(step == blocks - 1)
        def _():
            close_base()

        @pl.when(step >= LAG)
        def _():
            b = step - LAG

            @pl.when(receives)
            def _():
                for n in range(PARTS):
                    forward_copy(b * PARTS + n).wait_recv()

            second_half(b)

        @pl.when(step < blocks - 1)
        def _():
            pass_on(step * PARTS + 2)

    for d in range(1, npar):
        cpart_copy(d).wait()
    c_total = cpart_in[0]
    for q in range(1, npar):
        c_total = c_total + cpart_in[q]
    sums = [lane_sums(part[1 + g]) for g in range(2)]
    result = jnp.where(row == 0, sums[0], jnp.where(row == 1, sums[1], c_total))
    tot_out[...] = result
    tot_in[col] = result
    totals = []
    for d in range(1, ncol):
        copy = pltpu.make_async_remote_copy(
            src_ref=tot_out, dst_ref=tot_in.at[col],
            send_sem=t_ssem.at[d - 1], recv_sem=t_rsem.at[d - 1],
            device_id=(lax.rem(col + d, ncol), par), device_id_type=MESH,
        )
        copy.start()
        totals.append(copy)
    for d in range(1, npar):
        conc_copies[d - 1].wait_send()

    @pl.when(has_right)
    def _():
        wind_copy(0).wait_send()

    @pl.when(has_left)
    def _():
        wind_copy(1).wait_send()

    @pl.loop(0, chunks)
    def _(n):
        pair_copy(n, odd).wait_send()

        @pl.when(forwards)
        def _():
            forward_copy(n).wait_send()

    def find(k, found):
        return jnp.where(lane == order[0, k], k, found)

    place_row[...] = lax.fori_loop(0, species, find, jnp.zeros((SUB, 128), jnp.int32), unroll=16)[:1]
    placing = pltpu.make_async_copy(place_row, place, place_sem.at[0])
    placing.start()
    placing.wait()

    @pl.loop(0, species, unroll=32)
    def _(k):
        at = place[0, k]
        for g in range(2):
            news_ref[g, k] = news_rows[g, at]
        emis_rows[k] = newc_rows[at]

    turned = emis_rows.reshape(species * SUB, 128)
    for t in range(species // SUB):
        for r in range(rows):
            newc_ref[t * SUB:(t + 1) * SUB, r * 128:(r + 1) * 128] = turned[pl.ds(t * SUB * SUB + par * rows + r, SUB, stride=SUB), :]
    for copy in totals:
        copy.wait()
    total = tot_in[0]
    for q in range(1, ncol):
        total = total + tot_in[q]
    total = total / total_cells
    burd_ref[...] = total


def shards(
    concentration, emissions, rate_table, species_order, sensitivity, source_terms,
    courant_x, upwind_x, courant_y, upwind_y,
):
    ncol, npar = (lax.axis_size("cols"), lax.axis_size("params"))
    blocks, width = (rate_table.shape[0], rate_table.shape[1])
    groups, species, planes, layers, across = sensitivity.shape
    tall = planes * layers
    assert ncol % 2 == 0 and groups == 2 and tall == SUB and planes == 2 and across == 128
    cells = tall * across

    vm = pltpu.VMEM
    dma = pltpu.SemaphoreType.DMA
    in_vmem = pl.BlockSpec(memory_space=pltpu.VMEM)
    limits = pltpu.CompilerParams(vmem_limit_bytes=16 * 1024 * 1024)
    stacked = (groups, species, SUB, across)
    chunks = blocks * PARTS
    packed_shape = (chunks, width // PARTS, 2 * SUB, 128)
    newc_o, news_o, burd_o, order_o = pl.pallas_call(
        functools.partial(step_kernel, ncol, npar, blocks, width, cells * ncol),
        out_shape=(
            jax.ShapeDtypeStruct(concentration.shape, jnp.float32),
            jax.ShapeDtypeStruct(stacked, jnp.float32),
            jax.ShapeDtypeStruct((SUB, species), jnp.float32),
            jax.ShapeDtypeStruct((1, species), jnp.int32),
        ),
        in_specs=[pl.BlockSpec(memory_space=pltpu.HBM)] * 10,
        out_specs=[in_vmem] * 4,
        scratch_shapes=[
            pltpu.SMEM((1, species), jnp.int32),
            pltpu.SMEM(rate_table.shape, jnp.float32),
            vm(concentration.shape, jnp.float32),
            vm(concentration.shape, jnp.float32),
            vm(stacked, jnp.float32),
            vm(stacked, jnp.bfloat16),
            vm((SUB, 128), jnp.float32),
            vm((SUB, 128), jnp.int32),
            vm((SUB, 128), jnp.float32),
            vm((SUB, 128), jnp.int32),
            pltpu.SMEM((1, species), jnp.int32),
            vm((1, species), jnp.int32),
            vm((npar - 1,) + concentration.shape, jnp.float32),
            vm((species, SUB, 128), jnp.float32),
            vm((species, SUB, 128), jnp.float32),
            vm((species, SUB, 128), jnp.float32),
            vm(stacked, jnp.float32),
            vm((blocks, width, SUB, 128), jnp.float32),
            vm((blocks, width, width, SUB, 128), jnp.float32),
            vm((10, SUB, 128), jnp.float32),
            vm((2, SUB, 128), jnp.float32),
            vm((2, 2, SUB, 128), jnp.float32),
            vm(packed_shape, jnp.bfloat16),
            vm((2,) + packed_shape, jnp.bfloat16),
            vm((3, species, 128), jnp.float32),
            vm((SUB, species), jnp.float32),
            vm((npar, SUB, species), jnp.float32),
            vm((SUB, species), jnp.float32),
            vm((ncol, SUB, species), jnp.float32),
            dma((11,)),
            dma((1,)),
            dma((npar - 1,)), dma((npar - 1,)),
            dma((2,)), dma((2,)),
            dma((chunks,)), dma((chunks,)),
            dma((chunks,)), dma((chunks,)),
            dma((npar - 1,)), dma((npar - 1,)),
            dma((ncol - 1,)), dma((ncol - 1,)),
        ],
        compiler_params=pltpu.CompilerParams(
            collective_id=0, has_side_effects=True, vmem_limit_bytes=48 * 1024 * 1024
        ),
    )(
        pinned(species_order.reshape(1, species)), pinned(rate_table), pinned(concentration), pinned(emissions),
        pinned(sensitivity.reshape(stacked)), pinned(source_terms.reshape(stacked)),
        pinned(courant_x.reshape(SUB, across)), pinned(upwind_x.reshape(SUB, across)),
        pinned(courant_y.reshape(SUB, across)), pinned(upwind_y.reshape(SUB, across)),
    )
    newc, news, sburd, cburd = pl.pallas_call(
        write_kernel,
        out_shape=(
            jax.ShapeDtypeStruct(concentration.shape, jnp.float32),
            jax.ShapeDtypeStruct(stacked, jnp.float32),
            jax.ShapeDtypeStruct((groups, species), jnp.float32),
            jax.ShapeDtypeStruct((1, species), jnp.float32),
        ),
        in_specs=[in_vmem] * 4,
        out_specs=[pl.BlockSpec(memory_space=pltpu.HBM)] * 4,
        scratch_shapes=[
            vm((groups, species), jnp.float32),
            vm((1, species), jnp.float32),
            dma((4,)),
        ],
        compiler_params=limits,
    )(order_o, newc_o, news_o, burd_o)
    return (newc, news.reshape(sensitivity.shape), sburd, cburd.reshape(species))


def solution(mesh):
    in_specs = (
        P(None, ("cols", "params")),
        P(None, ("cols", "params")),
        P(),
        P(),
        P("params", None, "cols", None, None),
        P("params", None, "cols", None, None),
        P("cols", None, None),
        P("cols", None, None),
        P("cols", None, None),
        P("cols", None, None),
    )
    out_specs = (
        P(None, ("cols", "params")),
        P("params", None, "cols", None, None),
        P("params", None),
        P(),
    )
    return jax.shard_map(shards, mesh=mesh, in_specs=in_specs, out_specs=out_specs, check_vma=False)
```

```python
import functools
import jax
import jax.numpy as jnp
from jax import lax
from jax.experimental import pallas as pl
from jax.experimental.pallas import tpu as pltpu
from jax.sharding import PartitionSpec as P

MESH = pl.DeviceIdType.MESH
SUB = 8
PARTS = 2
LAG = 3


def pinned(value):
    return pltpu.with_memory_space_constraint(value, pltpu.HBM)


def write_kernel(order_row, newc_o, news_o, burd_o, newc_hbm, news_hbm, sburd_hbm, cburd_hbm, sburd, cburd, sems):
    species = newc_o.shape[0]
    held = ((news_o, news_hbm), (newc_o, newc_hbm), (sburd, sburd_hbm), (cburd, cburd_hbm))
    copies = [pltpu.make_async_copy(src, dst, sems.at[n]) for n, (src, dst) in enumerate(held)]
    for copy in copies[:2]:
        copy.start()
    at = lax.broadcasted_iota(jnp.int32, (species, species), 0)
    turn = jnp.where(at == order_row[...], 1.0, 0.0).astype(jnp.float32)
    total = lax.dot_general(
        burd_o[...], turn, (((1,), (1,)), ((), ())),
        precision=lax.Precision.HIGHEST, preferred_element_type=jnp.float32,
    )
    sburd[...] = total[:2]
    cburd[...] = total[2:3]
    for copy in copies[2:]:
        copy.start()
    for copy in copies:
        copy.wait()


def step_kernel(
    ncol, npar, blocks, width, total_cells,
    order_hbm, rate_hbm, conc_hbm, emis_hbm, sens_hbm, src_hbm, cx_hbm, ux_hbm, cy_hbm, uy_hbm,
    newc_ref, news_ref, burd_ref, order_out,
    order, rate, conc_ref, emis_ref, sens_ref, src_ref, cx_ref, ux_ref, cy_ref, uy_ref,
    place, place_row, conc_in, conc_rows, emis_rows, newc_rows, news_rows, invc, lu, coef, wind, wind_in,
    send, halo, part, cpart, cpart_in, tot_out, tot_in,
    known, in_sem, place_sem, conc_ssem, conc_rsem, w_ssem, w_rsem, p_ssem, p_rsem, f_ssem, f_rsem, cp_ssem, cp_rsem, t_ssem, t_rsem,
):
    species = blocks * width
    part_width = width // PARTS
    chunks = blocks * PARTS
    half = SUB // 2
    col, par = (lax.axis_index("cols"), lax.axis_index("params"))
    rows = conc_ref.shape[1] // 128
    has_left, has_right = (col > 0, col < ncol - 1)
    odd = lax.rem(col, 2)
    other = 1 - odd
    partner = col + 1 - 2 * odd
    ahead = col + 2 - 4 * odd
    forwards = jnp.logical_and(ahead >= 0, ahead < ncol)
    ahead = jnp.clip(ahead, 0, ncol - 1)
    behind = col - 2 + 4 * odd
    receives = jnp.logical_and(behind >= 0, behind < ncol)

    barrier = pltpu.get_barrier_semaphore()
    rounds = ncol.bit_length() - 1
    greeted = rounds + npar - 1
    for r in range(rounds):
        pl.semaphore_signal(barrier, inc=1, device_id=(jnp.bitwise_xor(col, 1 << r), par), device_id_type=MESH)
    for away in (-2, -1, 1, 2):
        there = jnp.logical_and(col + away >= 0, col + away < ncol)
        greeted = greeted + there.astype(jnp.int32)

        @pl.when(there)
        def _():
            pl.semaphore_signal(barrier, inc=1, device_id=(col + away, par), device_id_type=MESH)

    for d in range(1, npar):
        pl.semaphore_signal(barrier, inc=1, device_id=(col, lax.rem(par + d, npar)), device_id_type=MESH)

    held = (
        (order_hbm, order), (sens_hbm, sens_ref), (cx_hbm, cx_ref), (ux_hbm, ux_ref), (cy_hbm, cy_ref), (uy_hbm, uy_ref),
        (conc_hbm, conc_ref), (emis_hbm, emis_ref), (rate_hbm, rate), (src_hbm, src_ref), (order_hbm, order_out),
    )
    loads = [pltpu.make_async_copy(src, dst, in_sem.at[n]) for n, (src, dst) in enumerate(held)]
    for load in loads:
        load.start()

    row = lax.broadcasted_iota(jnp.int32, (SUB, 128), 0)
    lane = lax.broadcasted_iota(jnp.int32, (SUB, 128), 1)
    top = row < half

    @pl.when(jnp.logical_not(has_left))
    def _():
        halo[0] = jnp.zeros_like(halo[0])
        wind_in[0] = jnp.zeros_like(wind_in[0])

    @pl.when(jnp.logical_not(has_right))
    def _():
        halo[1] = jnp.zeros_like(halo[1])
        wind_in[1] = jnp.zeros_like(wind_in[1])

    def wind_copy(way):
        target = jnp.minimum(col + 1, ncol - 1) if way == 0 else jnp.maximum(col - 1, 0)
        return pltpu.make_async_remote_copy(
            src_ref=wind, dst_ref=wind_in.at[way], send_sem=w_ssem.at[way], recv_sem=w_rsem.at[way],
            device_id=(target, par), device_id_type=MESH,
        )

    def pair_copy(n, side):
        return pltpu.make_async_remote_copy(
            src_ref=send.at[n], dst_ref=halo.at[side, n], send_sem=p_ssem.at[n], recv_sem=p_rsem.at[n],
            device_id=(partner, par), device_id_type=MESH,
        )

    def forward_copy(n):
        return pltpu.make_async_remote_copy(
            src_ref=halo.at[other, n], dst_ref=halo.at[odd, n], send_sem=f_ssem.at[n], recv_sem=f_rsem.at[n],
            device_id=(ahead, par), device_id_type=MESH,
        )

    def pass_on(n):
        pair_copy(n, other).wait_recv()

        @pl.when(forwards)
        def _():
            forward_copy(n).start()

    def pack(n):
        for k in range(part_width):
            at = order[0, n * part_width + k]
            both = jnp.concatenate([sens_ref[0, at], sens_ref[1, at]], axis=0)
            send[n, k] = both.astype(jnp.bfloat16)

    for load in loads[2:6]:
        load.wait()
    wind[0] = jnp.where(ux_ref[...] == 1, cx_ref[...], -cx_ref[...])
    wind[1] = jnp.where(uy_ref[...] == 1, cy_ref[...], -cy_ref[...])
    loads[6].wait()
    loads[0].wait()
    loads[1].wait()
    pack(0)
    pl.semaphore_wait(barrier, greeted)

    def tell(r):
        pl.semaphore_signal(known.at[r], inc=1, device_id=(jnp.bitwise_xor(col, 1 << r), par), device_id_type=MESH)

    tell(0)
    conc_copies = []
    for d in range(1, npar):
        copy = pltpu.make_async_remote_copy(
            src_ref=conc_ref, dst_ref=conc_in.at[npar - 1 - d],
            send_sem=conc_ssem.at[d - 1], recv_sem=conc_rsem.at[npar - 1 - d],
            device_id=(col, lax.rem(par + d, npar)), device_id_type=MESH,
        )
        copy.start()
        conc_copies.append(copy)
    pair_copy(0, odd).start()

    @pl.when(has_right)
    def _():
        wind_copy(0).start()

    @pl.when(has_left)
    def _():
        wind_copy(1).start()

    @pl.loop(1, chunks)
    def _(n):
        pack(n)
        pair_copy(n, odd).start()

    def spread(read, target, base):
        target = target.reshape(species * SUB, 128)

        @pl.loop(0, species // SUB, unroll=8)
        def _(t):
            for r in range(rows):
                target[pl.ds(t * SUB * SUB + base + r, SUB, stride=SUB), :] = read(t, r)

    def own(ref):
        return lambda t, r: ref[pl.ds(pl.multiple_of(t * SUB, SUB), SUB), r * 128:(r + 1) * 128]

    spread(own(conc_ref), conc_rows, par * rows)
    loads[7].wait()
    spread(own(emis_ref), emis_rows, par * rows)
    for load in loads[8:]:
        load.wait()

    def set_coefficients():
        @pl.when(has_left)
        def _():
            wind_copy(0).wait_recv()

        @pl.when(has_right)
        def _():
            wind_copy(1).wait_recv()

        zero = jnp.zeros((SUB, 128), jnp.float32)

        def split(value):
            return (jnp.maximum(value, zero), jnp.maximum(-value, zero))

        def swap(value):
            return pltpu.roll(value, half, 0)

        def across(value):
            into, out = split(value)
            last = lane == 127
            next_in = jnp.where(last, zero, pltpu.roll(into, 127, 1))
            next_out = jnp.where(last, zero, pltpu.roll(out, 127, 1))
            return (out + next_in, jnp.where(lane == 0, zero, into), next_out)

        own_x, left_x, right_x = (wind[0], wind_in[0, 0], wind_in[1, 0])
        in_x, out_x = split(own_x)
        next_in, next_out = split(jnp.where(top, swap(own_x), swap(right_x)))
        lost, down, up = across(wind[1])
        coef[0] = 1.0 - (out_x + next_in) - lost
        coef[1] = jnp.where(jnp.logical_and(top, jnp.logical_not(has_left)), zero, in_x)
        coef[2] = next_out
        coef[3] = down
        coef[4] = up
        in_x, out_x = split(jnp.where(top, swap(left_x), swap(right_x)))
        next_in, next_out = split(jnp.where(top, own_x, right_x))
        lost, down, up = across(jnp.where(top, swap(wind_in[0, 1]), swap(wind_in[1, 1])))
        coef[5] = 1.0 - (out_x + next_in) - lost
        coef[6] = in_x
        coef[7] = next_out
        coef[8] = down
        coef[9] = up

    def stencil(first, value, before, after):
        a0, al, ar, ad, au = (coef[first + n] for n in range(5))
        return (
            a0 * value + al * before + ar * after
            + ad * pltpu.roll(value, 1, 1) + au * pltpu.roll(value, 127, 1)
        )

    def advance(s, h):
        turned = pltpu.roll(s, half, 0)
        return stencil(0, s, jnp.where(top, h, turned), jnp.where(top, turned, h))

    def transport(s, left, right):
        h = pltpu.roll(jnp.where(top, right, left), half, 0)
        next_h = stencil(5, h, jnp.where(top, left, s), jnp.where(top, s, right))
        return advance(advance(s, h), next_h)

    pass_on(0)
    for d in range(1, npar):
        conc_copies[npar - 1 - d].wait_recv()
        spread(own(conc_in.at[d - 1]), conc_rows, lax.rem(par + d, npar) * rows)

    set_coefficients()

    def factorize(b):
        c = [conc_rows[order[0, b * width + j]] for j in range(width)]
        for i in range(width):
            invc[b, i] = 1.0 / c[i]

        def fresh(i):
            rates = [rate[b, i, j] for j in range(width)]
            total = rates[0] * c[0]
            for j in range(1, width):
                total = total + rates[j] * c[j]
            diagonal = (1.0 + total) * invc[b, i] - rates[i]
            return [diagonal if j == i else jnp.full((SUB, 128), -rates[j], jnp.float32) for j in range(width)]

        for i in range(0, width, 2):
            x, y = (fresh(i), fresh(i + 1))
            for k in range(i):
                inv = lu[b, k, k]
                lx, ly = (x[k] * inv, y[k] * inv)
                lu[b, i, k] = lx
                lu[b, i + 1, k] = ly
                for j in range(k + 1, width):
                    u = lu[b, k, j]
                    x[j] = x[j] - lx * u
                    y[j] = y[j] - ly * u
            inv = 1.0 / x[i]
            lu[b, i, i] = inv
            ly = y[i] * inv
            lu[b, i + 1, i] = ly
            for j in range(i + 1, width):
                lu[b, i, j] = x[j]
                y[j] = y[j] - ly * x[j]
            lu[b, i + 1, i + 1] = 1.0 / y[i + 1]
            for j in range(i + 2, width):
                lu[b, i + 1, j] = y[j]

    def solve(b, sides):
        sides = [list(side) for side in sides]
        for k in range(width):
            for i in range(k + 1, width):
                low = lu[b, i, k]
                for side in sides:
                    side[i] = side[i] - low * side[k]
        for k in range(width - 1, -1, -1):
            inv = lu[b, k, k]
            for side in sides:
                side[k] = side[k] * inv
            for i in range(k):
                up = lu[b, i, k]
                for side in sides:
                    side[i] = side[i] - up * side[k]
        return [[side[k] * invc[b, k] for k in range(width)] for side in sides]

    def first_half(b):
        factorize(b)
        base = []
        for k in range(width):
            at = order[0, b * width + k]
            base.append(conc_rows[at] + emis_rows[at])
        (base,) = solve(b, [base])
        for k in range(width):
            o = b * width + k
            newc_rows[o] = base[k]

    def second_half(b):
        sides = [[], []]
        for k in range(width):
            at = order[0, b * width + k]
            n, m = (b * PARTS + k // part_width, k % part_width)
            left, right = (halo[0, n, m].astype(jnp.float32), halo[1, n, m].astype(jnp.float32))
            for g in range(2):
                rows_g = slice(g * SUB, (g + 1) * SUB)
                moved = transport(sens_ref[g, at], left[rows_g], right[rows_g])
                sides[g].append(moved + src_ref[g, at].astype(jnp.float32))
        sides = solve(b, sides)
        for g in range(2):
            for k in range(width):
                news_rows[g, b * width + k] = sides[g][k]
        flat = news_rows.reshape(2 * species * SUB, 128)
        for g in range(2):
            for t in range(width // SUB):
                first = b * width + t * SUB
                total = jnp.zeros((SUB, 128), jnp.float32)
                for r in range(SUB):
                    total = total + flat[pl.ds((g * species + first) * SUB + r, SUB, stride=SUB), :]
                part[1 + g, pl.ds(pl.multiple_of(first, SUB), SUB), :] = total

    ones = jnp.ones((SUB, 128), jnp.bfloat16)

    def lane_sums(value):
        high = value.astype(jnp.bfloat16)
        low = (value - high.astype(jnp.float32)).astype(jnp.bfloat16)
        both = [
            lax.dot_general(ones, piece, (((1,), (1,)), ((), ())), preferred_element_type=jnp.float32)
            for piece in (high, low)
        ]
        return both[0] + both[1]

    def cpart_copy(d):
        return pltpu.make_async_remote_copy(
            src_ref=cpart, dst_ref=cpart_in.at[par],
            send_sem=cp_ssem.at[d - 1], recv_sem=cp_rsem.at[d - 1],
            device_id=(col, lax.rem(par + d, npar)), device_id_type=MESH,
        )

    def close_base():
        @pl.loop(0, species // SUB, unroll=8)
        def _(t):
            total = jnp.zeros((SUB, 128), jnp.float32)
            at = pl.ds(pl.multiple_of(t * SUB, SUB), SUB)
            for r in range(rows):
                total = total + newc_rows.reshape(species * SUB, 128)[pl.ds(t * SUB * SUB + par * rows + r, SUB, stride=SUB), :]
            part[0, at, :] = total

        own_c = lane_sums(part[0])
        cpart[...] = own_c
        cpart_in[par] = own_c

        for d in range(1, npar):
            cpart_copy(d).start()

    @pl.loop(0, blocks + LAG)
    def _(step):
        @pl.when(step < blocks)
        def _():
            first_half(step)
            pass_on(step * PARTS + 1)

        for r in range(rounds):
            @pl.when(step == blocks - rounds + r)
            def _():
                pl.semaphore_wait(known.at[r], 1)
                if r + 1 < rounds:
                    tell(r + 1)

        @pl.when(step == blocks - 1)
        def _():
            close_base()

        @pl.when(step >= LAG)
        def _():
            b = step - LAG

            @pl.when(receives)
            def _():
                for n in range(PARTS):
                    forward_copy(b * PARTS + n).wait_recv()

            second_half(b)

        @pl.when(step < blocks - 1)
        def _():
            pass_on(step * PARTS + 2)

    for d in range(1, npar):
        cpart_copy(d).wait()
    c_total = cpart_in[0]
    for q in range(1, npar):
        c_total = c_total + cpart_in[q]
    sums = [lane_sums(part[1 + g]) for g in range(2)]
    result = jnp.where(row == 0, sums[0], jnp.where(row == 1, sums[1], c_total))
    tot_out[...] = result
    tot_in[col] = result
    totals = []
    for d in range(1, ncol):
        copy = pltpu.make_async_remote_copy(
            src_ref=tot_out, dst_ref=tot_in.at[col],
            send_sem=t_ssem.at[d - 1], recv_sem=t_rsem.at[d - 1],
            device_id=(lax.rem(col + d, ncol), par), device_id_type=MESH,
        )
        copy.start()
        totals.append(copy)
    for d in range(1, npar):
        conc_copies[d - 1].wait_send()

    @pl.when(has_right)
    def _():
        wind_copy(0).wait_send()

    @pl.when(has_left)
    def _():
        wind_copy(1).wait_send()

    @pl.loop(0, chunks)
    def _(n):
        pair_copy(n, odd).wait_send()

        @pl.when(forwards)
        def _():
            forward_copy(n).wait_send()

    def find(k, found):
        return jnp.where(lane == order[0, k], k, found)

    place_row[...] = lax.fori_loop(0, species, find, jnp.zeros((SUB, 128), jnp.int32), unroll=16)[:1]
    placing = pltpu.make_async_copy(place_row, place, place_sem.at[0])
    placing.start()
    placing.wait()

    @pl.loop(0, species, unroll=32)
    def _(k):
        at = place[0, k]
        for g in range(2):
            news_ref[g, k] = news_rows[g, at]
        emis_rows[k] = newc_rows[at]

    turned = emis_rows.reshape(species * SUB, 128)
    for t in range(species // SUB):
        for r in range(rows):
            newc_ref[t * SUB:(t + 1) * SUB, r * 128:(r + 1) * 128] = turned[pl.ds(t * SUB * SUB + par * rows + r, SUB, stride=SUB), :]
    for copy in totals:
        copy.wait()
    total = tot_in[0]
    for q in range(1, ncol):
        total = total + tot_in[q]
    total = total / total_cells
    burd_ref[...] = total


def shards(
    concentration, emissions, rate_table, species_order, sensitivity, source_terms,
    courant_x, upwind_x, courant_y, upwind_y,
):
    ncol, npar = (lax.axis_size("cols"), lax.axis_size("params"))
    blocks, width = (rate_table.shape[0], rate_table.shape[1])
    groups, species, planes, layers, across = sensitivity.shape
    tall = planes * layers
    assert ncol >= 2 and ncol & (ncol - 1) == 0 and groups == 2 and tall == SUB and planes == 2 and across == 128
    cells = tall * across

    vm = pltpu.VMEM
    dma = pltpu.SemaphoreType.DMA
    in_vmem = pl.BlockSpec(memory_space=pltpu.VMEM)
    limits = pltpu.CompilerParams(vmem_limit_bytes=16 * 1024 * 1024)
    stacked = (groups, species, SUB, across)
    chunks = blocks * PARTS
    packed_shape = (chunks, width // PARTS, 2 * SUB, 128)
    newc_o, news_o, burd_o, order_o = pl.pallas_call(
        functools.partial(step_kernel, ncol, npar, blocks, width, cells * ncol),
        out_shape=(
            jax.ShapeDtypeStruct(concentration.shape, jnp.float32),
            jax.ShapeDtypeStruct(stacked, jnp.float32),
            jax.ShapeDtypeStruct((SUB, species), jnp.float32),
            jax.ShapeDtypeStruct((1, species), jnp.int32),
        ),
        in_specs=[pl.BlockSpec(memory_space=pltpu.HBM)] * 10,
        out_specs=[in_vmem] * 4,
        scratch_shapes=[
            pltpu.SMEM((1, species), jnp.int32),
            pltpu.SMEM(rate_table.shape, jnp.float32),
            vm(concentration.shape, jnp.float32),
            vm(concentration.shape, jnp.float32),
            vm(stacked, jnp.float32),
            vm(stacked, jnp.bfloat16),
            vm((SUB, 128), jnp.float32),
            vm((SUB, 128), jnp.int32),
            vm((SUB, 128), jnp.float32),
            vm((SUB, 128), jnp.int32),
            pltpu.SMEM((1, species), jnp.int32),
            vm((1, species), jnp.int32),
            vm((npar - 1,) + concentration.shape, jnp.float32),
            vm((species, SUB, 128), jnp.float32),
            vm((species, SUB, 128), jnp.float32),
            vm((species, SUB, 128), jnp.float32),
            vm(stacked, jnp.float32),
            vm((blocks, width, SUB, 128), jnp.float32),
            vm((blocks, width, width, SUB, 128), jnp.float32),
            vm((10, SUB, 128), jnp.float32),
            vm((2, SUB, 128), jnp.float32),
            vm((2, 2, SUB, 128), jnp.float32),
            vm(packed_shape, jnp.bfloat16),
            vm((2,) + packed_shape, jnp.bfloat16),
            vm((3, species, 128), jnp.float32),
            vm((SUB, species), jnp.float32),
            vm((npar, SUB, species), jnp.float32),
            vm((SUB, species), jnp.float32),
            vm((ncol, SUB, species), jnp.float32),
            pltpu.SemaphoreType.REGULAR((ncol.bit_length() - 1,)),
            dma((11,)),
            dma((1,)),
            dma((npar - 1,)), dma((npar - 1,)),
            dma((2,)), dma((2,)),
            dma((chunks,)), dma((chunks,)),
            dma((chunks,)), dma((chunks,)),
            dma((npar - 1,)), dma((npar - 1,)),
            dma((ncol - 1,)), dma((ncol - 1,)),
        ],
        compiler_params=pltpu.CompilerParams(
            collective_id=0, has_side_effects=True, vmem_limit_bytes=48 * 1024 * 1024
        ),
    )(
        pinned(species_order.reshape(1, species)), pinned(rate_table), pinned(concentration), pinned(emissions),
        pinned(sensitivity.reshape(stacked)), pinned(source_terms.reshape(stacked)),
        pinned(courant_x.reshape(SUB, across)), pinned(upwind_x.reshape(SUB, across)),
        pinned(courant_y.reshape(SUB, across)), pinned(upwind_y.reshape(SUB, across)),
    )
    newc, news, sburd, cburd = pl.pallas_call(
        write_kernel,
        out_shape=(
            jax.ShapeDtypeStruct(concentration.shape, jnp.float32),
            jax.ShapeDtypeStruct(stacked, jnp.float32),
            jax.ShapeDtypeStruct((groups, species), jnp.float32),
            jax.ShapeDtypeStruct((1, species), jnp.float32),
        ),
        in_specs=[in_vmem] * 4,
        out_specs=[pl.BlockSpec(memory_space=pltpu.HBM)] * 4,
        scratch_shapes=[
            vm((groups, species), jnp.float32),
            vm((1, species), jnp.float32),
            dma((4,)),
        ],
        compiler_params=limits,
    )(order_o, newc_o, news_o, burd_o)
    return (newc, news.reshape(sensitivity.shape), sburd, cburd.reshape(species))


def solution(mesh):
    in_specs = (
        P(None, ("cols", "params")),
        P(None, ("cols", "params")),
        P(),
        P(),
        P("params", None, "cols", None, None),
        P("params", None, "cols", None, None),
        P("cols", None, None),
        P("cols", None, None),
        P("cols", None, None),
        P("cols", None, None),
    )
    out_specs = (
        P(None, ("cols", "params")),
        P("params", None, "cols", None, None),
        P("params", None),
        P(),
    )
    return jax.shard_map(shards, mesh=mesh, in_specs=in_specs, out_specs=out_specs, check_vma=False)
```
